256 devices in a mesh: dp: 4 (over x), seq: 64 (over z, y, core).
Axes of the slice: x: 4, y: 4, z: 8, core: 2. Of those that a mesh axis runs over, the one named last changes fastest.
Arguments:
- streams: bfloat16 [3, 4, 8192, 4096], P(None, 'dp', 'seq'), may hold values from -6 to 6
- short_filter: float32 [3, 3, 4096], P(None, None, 'dp'), may hold values from -3.5 to 3.5
- decay_rate: float32 [2, 4096], P(None, 'dp'), may hold values from 1.2207031e-06 to 0.05
- pole_angle: float32 [2, 4096], P(None, 'dp'), may hold values from -3.140625 to 3.140625
- residue_re: float32 [2, 4096], P(None, 'dp'), may hold values from -6 to 6
- residue_im: float32 [2, 4096], P(None, 'dp'), may hold values from -6 to 6
- skip_gain: float32 [4096], P('dp'), may hold values from -6 to 6
- doc_starts: int32 [4, 8], P('dp'), may hold values from 0 to 8191, as said below
Outputs:
- mixed: bfloat16 [4, 8192, 4096], P('dp', 'seq')
The draws below stay inside these ranges and needn't reach their ends.
Inputs may be any that keep to these rules, and one draw needn't show every extreme that they name: `doc_starts`: each row starts with 0 and rises strictly; the last document of every sequence is one position long.
All inputs are finite; a program needn't handle non-finite values.
Results may differ from the reference program's by a relative error of at most 0.0045.
Values may be sent and summed in bfloat16 or wider, within the bound.
A program may use at most 128 MiB of HBM per device.

```python
import math
import jax
import jax.numpy as jnp
from jax import lax

CH = 4096
MODES = 2
TOK_DEV = 128
DOCS = 8
SEQS = 4
SEQ_LEN = 8192
N_SEQ = 64


def draw_doc_starts(key, part):
    total = TOK_DEV * N_SEQ
    seq_keys = jax.random.split(key, SEQS)

    def one_row(row_key):
        picks = jax.random.permutation(row_key, total - 2)[:DOCS - 2] + 1
        return jnp.concatenate([jnp.zeros((1,), jnp.int32), jnp.sort(picks).astype(jnp.int32), jnp.full((1,), total - 1, jnp.int32)])
    return jax.vmap(one_row)(seq_keys)


def block_scale(rng, shape, cuts, smallest, top_value):
    gain, own = 1.0, jax.random.fold_in(rng, 6)
    for position, shards_of in cuts:
        heights = jnp.exp(jax.random.uniform(jax.random.fold_in(own, position), (shards_of,), jnp.float32, smallest / len(cuts), top_value / len(cuts)))
        gain = gain * jnp.repeat(heights, shape[position] // shards_of).reshape([-1 if axis == position else 1 for axis in range(len(shape))])
    return gain


def noise(rng, dims, deviation, most, shards=(), held_as=jnp.bfloat16):
    values = deviation * jax.random.normal(rng, dims, jnp.float32)
    if shards:
        values = values * block_scale(rng, dims, shards, -0.22, 0.18)
    return jnp.clip(values, -most, most).astype(held_as)


def setup_inputs(seed: int = 0) -> dict:
    streams_of = jax.random.split(jax.random.key(seed), 9)
    streams = noise(streams_of[0], (3, SEQS, SEQ_LEN, CH), 1.0, 6.0, ((1, 4), (2, 64)))
    short_filter = noise(streams_of[1], (3, 3, CH), 3 ** -0.5, 3.5, ((2, 4),), jnp.float32)
    decay_rate = jnp.clip(jnp.exp(math.log(0.05) - 10.620351 * jax.random.uniform(streams_of[2], (MODES, CH), jnp.float32) ** block_scale(streams_of[2], (MODES, CH), ((1, 4),), -0.2, 0.2)), 1.220703097715159e-06, 0.05)
    pole_angle = jnp.clip(jax.random.uniform(streams_of[3], (MODES, CH), jnp.float32, -3.140625, 3.140625), -3.140625, 3.140625)
    residue_re = noise(streams_of[4], (MODES, CH), 1.0, 6.0, ((1, 4),), jnp.float32)
    residue_im = noise(streams_of[5], (MODES, CH), 1.0, 6.0, ((1, 4),), jnp.float32)
    skip_gain = noise(streams_of[6], (CH,), 1.0, 6.0, ((0, 4),), jnp.float32)
    doc_starts = draw_doc_starts(jax.random.fold_in(streams_of[8], 71), 0)
    return {"streams": streams, "short_filter": short_filter, "decay_rate": decay_rate, "pole_angle": pole_angle, "residue_re": residue_re, "residue_im": residue_im, "skip_gain": skip_gain, "doc_starts": doc_starts}


def reference(streams, short_filter, decay_rate, pole_angle, residue_re, residue_im, skip_gain, doc_starts):
    magnitude = jnp.exp(-decay_rate)
    pole_re = magnitude * jnp.cos(pole_angle)
    pole_im = magnitude * jnp.sin(pole_angle)
    norm_factor = jnp.sqrt(-jnp.expm1(-2.0 * decay_rate))
    weight_re = norm_factor * residue_re
    weight_im = norm_factor * residue_im
    seq_length = streams.shape[2]
    positions = jnp.arange(seq_length, dtype=jnp.int32)

    def one_sequence(packed):
        seq_index, starts = packed
        seq_streams = lax.dynamic_index_in_dim(streams, seq_index, 1, keepdims=False).astype(jnp.float32)
        padded = jnp.pad(seq_streams, ((0, 0), (2, 0), (0, 0)))
        filtered = short_filter[0][:, None, :] * padded[:, 2:] + short_filter[1][:, None, :] * padded[:, 1:-1] + short_filter[2][:, None, :] * padded[:, :-2]
        product = filtered[0] * filtered[1]
        keep_flag = 1.0 - jnp.any(positions[:, None] == starts[None, :], axis=1).astype(jnp.float32)

        def advance(running, inputs):
            state_re, state_im = running
            value_row, kept_now = inputs
            new_re = kept_now * (pole_re * state_re - pole_im * state_im) + value_row
            new_im = kept_now * (pole_re * state_im + pole_im * state_re)
            emitted = lax.optimization_barrier(jnp.sum(weight_re * new_re - weight_im * new_im, axis=0))
            return ((new_re, new_im), emitted)
        zero_state = jnp.zeros(decay_rate.shape, jnp.float32)
        final_state, long_part = lax.scan(advance, (zero_state, zero_state), (product, keep_flag))
        response = skip_gain * product + long_part
        return (filtered[2] * response).astype(jnp.bfloat16)
    seq_ids = jnp.arange(streams.shape[1], dtype=jnp.int32)
    return lax.map(one_sequence, (seq_ids, doc_starts))
```

```python
import functools

import jax
import jax.numpy as jnp
from jax import lax
from jax.experimental import pallas as pl
from jax.experimental.pallas import tpu as pltpu
from jax.sharding import PartitionSpec as P

MESH = pl.DeviceIdType.MESH
F32 = jnp.float32
BF16 = jnp.bfloat16
LANES = 128
CHUNKS = 8
STEPS = 16
TOK = CHUNKS * STEPS


def iota(shape, axis):
    return lax.broadcasted_iota(jnp.int32, shape, axis)


def rows(ref, row, count=8):
    return jnp.broadcast_to(ref[pl.ds(row, 1), :], (count, LANES))


def cmul(ar, ai, br, bi):
    return ar * br - ai * bi, ar * bi + ai * br


def kernel(
    n_dp,
    n_seq,
    plane,
    streams_hbm,
    taps_hbm,
    decay_hbm,
    angle_hbm,
    resr_hbm,
    resi_hbm,
    skip_hbm,
    starts_hbm,
    out_hbm,
    xbuf,
    hsend,
    hrecv,
    taps_v,
    decay_v,
    angle_v,
    resr_v,
    resi_v,
    skip_v,
    raw,
    starts_s,
    par_a,
    par_b,
    derived,
    perm_in,
    perm_out,
    m_keep,
    m_tail,
    m_first,
    m_scan,
    m_dev,
    vbuf,
    gr,
    gm,
    excl,
    table,
    state,
    r1,
    pre,
    total,
    r2,
    back,
    inflow,
    obuf,
    in_sem,
    x_sem,
    pa_send,
    pa_recv,
    pb_send,
    pb_recv,
    h_send,
    h_recv,
    s1_send,
    s1_recv,
    s2_send,
    s2_recv,
    s3_send,
    s3_recv,
    o_sem,
):
    n_z = n_seq // plane
    width = plane * LANES
    me_x = lax.axis_index("dp")
    me = lax.axis_index("seq")
    me_z = me // plane
    me_q = me % plane
    offsets = [0]
    for d in range(1, n_dp // 2 + 1):
        offsets.append(d)
        if n_dp - d != d:
            offsets.append(n_dp - d)

    x_peer = [None] + [((me_x + n_dp - o) % n_dp, me) for o in offsets[1:]]
    q_rank = [(me_q + k) % plane for k in range(1, plane)]
    q_peer = [(me_x, me_z * plane + r) for r in q_rank]
    z_peer = [(me_x, ((me_z + k) % n_z) * plane + me_q) for k in range(1, n_z)]
    after = (me_x, (me + 1) % n_seq)
    before = (me_x, (me + n_seq - 1) % n_seq)
    block = [(me_x + o) % n_dp for o in offsets]

    barrier = pltpu.get_barrier_semaphore()
    peers = x_peer[1:] + q_peer + z_peer + [after, before]
    for peer in peers:
        pl.semaphore_signal(barrier, inc=1, device_id=peer, device_id_type=MESH)

    loads = [
        pltpu.make_async_copy(a, b, in_sem.at[n])
        for n, (a, b) in enumerate(
            [
                (taps_hbm, taps_v),
                (decay_hbm, decay_v),
                (angle_hbm, angle_v),
                (resr_hbm, resr_v),
                (resi_hbm, resi_v),
                (skip_hbm, skip_v),
                (starts_hbm, starts_s),
            ]
        )
    ]
    for copy in loads:
        copy.start()
    x_loads = []
    for j in range(n_dp):
        columns = pl.ds(pl.multiple_of(block[j] * width, width), width)
        copy = pltpu.make_async_copy(streams_hbm.at[:, 0, :, columns], xbuf.at[j], x_sem.at[j])
        copy.start()
        x_loads.append(copy)

    lines = TOK + 16
    row = iota((lines, lines), 0)
    col = iota((lines, lines), 1)
    place = (row % CHUNKS) * STEPS + row // CHUNKS - 2
    has_before = jnp.where(me > 0, 1, 0)
    for s in range(3):
        pick = jnp.where(place >= 0, place, jnp.where(has_before > 0, TOK + 2 * s + 2 + place, -1))
        perm_in[s] = jnp.where(col == pick, 1.0, 0.0).astype(BF16)
    row = iota((TOK, TOK), 0)
    col = iota((TOK, TOK), 1)
    perm_out[...] = jnp.where(col == (row % STEPS) * CHUNKS + row // STEPS, 1.0, 0.0).astype(BF16)

    for copy in loads[:6]:
        copy.wait()
    for i in range(plane):
        lane = slice(i * LANES, (i + 1) * LANES)
        for s in range(2):
            for k in range(3):
                par_a[0, (3 * s + k) * plane + i, :] = taps_v[k, s, lane]
        for k in range(3):
            par_b[0, k * plane + i, :] = taps_v[k, 2, lane]
        par_b[0, 7 * plane + i, :] = skip_v[0, lane]
        for m in range(2):
            r = 2 * i + m
            for n, source in enumerate((decay_v, angle_v, resr_v, resi_v)):
                raw[n, r, :] = source[m, lane]
    decay = raw[0]
    magnitude = jnp.exp(-decay)
    par_a[0, 6 * plane : 8 * plane, :] = magnitude * jnp.cos(raw[1])
    par_a[0, 8 * plane : 10 * plane, :] = magnitude * jnp.sin(raw[1])
    square = decay * decay
    sinh = decay * (1.0 + square * (1.0 / 6.0) * (1.0 + square * (1.0 / 20.0) * (1.0 + square * (1.0 / 42.0))))
    norm = jnp.sqrt(2.0 * magnitude * sinh)
    par_b[0, 3 * plane : 5 * plane, :] = norm * raw[2]
    par_b[0, 5 * plane : 7 * plane, :] = norm * raw[3]

    row = iota((16, 16), 0)
    col = iota((16, 16), 1)
    for j in range(n_dp):
        x_loads[j].wait()
        for n in range(width // 256):
            lane = slice(n * 256, (n + 1) * 256)
            rim = jnp.zeros((16, 256), F32)
            for s in range(3):
                pick = jnp.where((row // 2 == s) & (col == 14 + row % 2), 1.0, 0.0).astype(BF16)
                rim += jnp.dot(pick, xbuf[j, s, TOK - 16 :, lane], preferred_element_type=F32)
            hsend[j, :, lane] = rim.astype(BF16)

    pl.semaphore_wait(barrier, len(peers))

    sends = []

    def send(source, target, send_sem, recv_sem, device):
        copy = pltpu.make_async_remote_copy(
            src_ref=source, dst_ref=target, send_sem=send_sem, recv_sem=recv_sem, device_id=device, device_id_type=MESH
        )
        copy.start()
        sends.append(copy)
        return copy

    a_copies = [None] + [
        send(par_a.at[0], par_a.at[j], pa_send.at[j], pa_recv.at[j], x_peer[j]) for j in range(1, n_dp)
    ]
    h_copies = [send(hsend.at[j], hrecv.at[j], h_send.at[j], h_recv.at[j], after) for j in range(n_dp)]
    b_copies = [None] + [
        send(par_b.at[0], par_b.at[j], pb_send.at[j], pb_recv.at[j], x_peer[j]) for j in range(1, n_dp)
    ]

    loads[6].wait()
    starts = [starts_s[0, d] for d in range(starts_s.shape[1])]
    near = [s - me * TOK for s in starts]
    chunk = iota((8, LANES), 0)
    one = jnp.ones((8, LANES), F32)
    zero = jnp.zeros((8, LANES), F32)

    def free(lo, hi, among):
        hit = (among[0] >= lo) & (among[0] < hi)
        for s in among[1:]:
            hit = hit | ((s >= lo) & (s < hi))
        return jnp.where(hit, zero, one)

    for k in range(STEPS):
        here = chunk * STEPS + k
        m_keep[k] = free(here, here + 1, near)
        m_tail[k] = free(here + 1, chunk * STEPS + STEPS, near)
        m_first[k] = free(jnp.zeros_like(here), here + 1, near)
    for n, shift in enumerate((1, 2, 4)):
        reach = free((chunk - shift + 1) * STEPS, (chunk + 1) * STEPS, near)
        m_scan[n] = jnp.where(chunk >= shift, reach, zero)
    first_of_plane = me_z * plane * TOK
    m_dev[0] = free(first_of_plane + chunk * TOK, first_of_plane + (chunk + 1) * TOK, starts)
    m_dev[1] = free(chunk * plane * TOK, (chunk + 1) * plane * TOK, starts)

    n_rows = 2 * plane
    log_plane = plane.bit_length() - 1

    def filters(j, s, i, source, base, x):
        c = [rows(source.at[j], (base + k) * plane + i) for k in range(3)]
        return [c[0] * x[k + 2] + c[1] * x[k + 1] + c[2] * x[k] for k in range(STEPS)]

    def permuted(j, s, i2):
        lane = pl.ds(pl.multiple_of(i2 * 256, 256), 256)
        operand = jnp.concatenate([xbuf[j, s, :, lane], hrecv[j, :, lane]], axis=0)
        return jnp.dot(perm_in[s], operand, preferred_element_type=F32)

    def half(x, h):
        return [x[8 * g : 8 * g + 8, h * LANES : (h + 1) * LANES] for g in range(STEPS + 2)]

    def states(j):
        pr = par_a[j, 6 * plane : 8 * plane, :]
        pi = par_a[j, 8 * plane : 10 * plane, :]
        qr, qi = pr, pi
        slot = 0
        for n in range(7 + log_plane):
            qr, qi = qr * qr - qi * qi, 2.0 * qr * qi
            if n + 1 in (4, 5, 6, 7, 7 + log_plane):
                derived[j, slot * n_rows : (slot + 1) * n_rows, :] = qr
                derived[j, (slot + 1) * n_rows : (slot + 2) * n_rows, :] = qi
                slot += 2
        derived[j, 10 * n_rows : 11 * n_rows, :] = 2.0 * pr
        derived[j, 11 * n_rows : 12 * n_rows, :] = pr * pr + pi * pi

        @pl.loop(0, width // 256)
        def _(i2):
            x0 = permuted(j, 0, i2)
            x1 = permuted(j, 1, i2)
            for h in range(2):
                i = 2 * i2 + h
                f0 = filters(j, 0, i, par_a, 0, half(x0, h))
                f1 = filters(j, 1, i, par_a, 3, half(x1, h))
                v = [a * b for a, b in zip(f0, f1)]
                for k in range(STEPS):
                    vbuf[j, i, 8 * k : 8 * k + 8, :] = v[k]
                masked = [v[k] * m_tail[k] for k in range(STEPS)]
                for m in range(2):
                    r = 2 * i + m
                    a1 = rows(derived.at[j], 10 * n_rows + r)
                    a2 = rows(derived.at[j], 11 * n_rows + r)
                    b1, b2 = masked[0], zero
                    for k in range(1, STEPS):
                        b1, b2 = a1 * b1 + (masked[k] - a2 * b2), b1
                    er = b1 - rows(par_a.at[j], 6 * plane + r) * b2
                    ei = rows(par_a.at[j], 8 * plane + r) * b2
                    for n, shift in enumerate((1, 2, 4)):
                        reach = m_scan[n]
                        kr = reach * rows(derived.at[j], 2 * n * n_rows + r)
                        ki = reach * rows(derived.at[j], (2 * n + 1) * n_rows + r)
                        sr = pltpu.roll(er, shift, axis=0)
                        si = pltpu.roll(ei, shift, axis=0)
                        ar, ai = cmul(kr, ki, sr, si)
                        er, ei = er + ar, ei + ai
                    state[j, i, pl.ds(m, 1), :] = er[7:8]
                    state[j, i, pl.ds(2 + m, 1), :] = ei[7:8]
                    later = jnp.where(chunk >= 1, one, zero)
                    excl[j, i, 16 * m : 16 * m + 8, :] = pltpu.roll(er, 1, axis=0) * later
                    excl[j, i, 16 * m + 8 : 16 * m + 16, :] = pltpu.roll(ei, 1, axis=0) * later

    def gather_plane(j):
        r1[j, me_q] = state[j, me_q]
        return [
            send(state.at[j, q_rank[n]], r1.at[j, me_q], s1_send.at[j, n], s1_recv.at[j, n], q_peer[n])
            for n in range(plane - 1)
        ]

    def combine_plane(j, copies):
        for copy in copies:
            copy.wait_recv()
        pr = derived[j, pl.ds(6 * n_rows + 2 * me_q, 2), :]
        pi = derived[j, pl.ds(7 * n_rows + 2 * me_q, 2), :]
        run_r = jnp.zeros((2, LANES), F32)
        run_i = run_r
        for e in range(plane):
            pre[j, e, 0:2, :] = run_r
            pre[j, e, 2:4, :] = run_i
            keep = m_dev[0, e : e + 1, :]
            ar, ai = cmul(pr * keep, pi * keep, run_r, run_i)
            run_r = ar + r1[j, e, 0:2, :]
            run_i = ai + r1[j, e, 2:4, :]
        total[j, 0:2, :] = run_r
        total[j, 2:4, :] = run_i
        r2[j, me_z] = total[j]
        return [
            send(total.at[j], r2.at[j, me_z], s2_send.at[j, n], s2_recv.at[j, n], z_peer[n]) for n in range(n_z - 1)
        ]

    def combine_all(j, copies):
        for copy in copies:
            copy.wait_recv()
        pr = derived[j, pl.ds(8 * n_rows + 2 * me_q, 2), :]
        pi = derived[j, pl.ds(9 * n_rows + 2 * me_q, 2), :]
        run_r = jnp.zeros((2, LANES), F32)
        run_i = run_r
        for z in range(n_z - 1):
            keep = m_dev[1, z : z + 1, :]
            ar, ai = cmul(pr * keep, pi * keep, run_r, run_i)
            past = z < me_z
            run_r = jnp.where(past, ar + r2[j, z, 0:2, :], run_r)
            run_i = jnp.where(past, ai + r2[j, z, 2:4, :], run_i)
        pr = derived[j, pl.ds(6 * n_rows + 2 * me_q, 2), :]
        pi = derived[j, pl.ds(7 * n_rows + 2 * me_q, 2), :]
        for e in range(plane):
            back[j, e, 0:2, :] = pre[j, e, 0:2, :] + run_r
            back[j, e, 2:4, :] = pre[j, e, 2:4, :] + run_i
            keep = m_dev[0, e : e + 1, :]
            run_r, run_i = cmul(pr * keep, pi * keep, run_r, run_i)
        inflow[j, me_q] = back[j, me_q]
        return [
            send(back.at[j, q_rank[n]], inflow.at[j, me_q], s3_send.at[j, n], s3_recv.at[j, n], q_peer[n])
            for n in range(plane - 1)
        ]

    def response(j):
        @pl.loop(0, width // 256)
        def _(i2):
            x2 = permuted(j, 2, i2)
            for h in range(2):
                i = 2 * i2 + h
                gate = filters(j, 2, i, par_b, 0, half(x2, h))
                skip = rows(par_b.at[j], 7 * plane + i)
                v = [vbuf[j, i, 8 * k : 8 * k + 8, :] for k in range(STEPS)]
                y = [skip * v[k] for k in range(STEPS)]
                for m in range(2):
                    r = 2 * i + m
                    pr = rows(par_a.at[j], 6 * plane + r)
                    pi = rows(par_a.at[j], 8 * plane + r)
                    wr = rows(par_b.at[j], 3 * plane + r)
                    wi = rows(par_b.at[j], 5 * plane + r)
                    sr = excl[j, i, 16 * m : 16 * m + 8, :]
                    si = excl[j, i, 16 * m + 8 : 16 * m + 16, :]
                    for k in range(STEPS):
                        keep = m_keep[k]
                        tr, ti = keep * sr, keep * si
                        sr = pr * tr - pi * ti + v[k]
                        si = pr * ti + pi * tr
                        y[k] = y[k] + (wr * sr - wi * si)
                    for n, bit in enumerate((1, 2, 4)):
                        on = (chunk & bit) > 0
                        br = jnp.where(on, rows(derived.at[j], 2 * n * n_rows + r), one)
                        bi = jnp.where(on, rows(derived.at[j], (2 * n + 1) * n_rows + r), zero)
                        wr, wi = cmul(wr, wi, br, bi)
                    table[j, i, 32 * m : 32 * m + 8, :] = wr
                    table[j, i, 32 * m + 8 : 32 * m + 16, :] = wi
                    wr, wi = cmul(wr, wi, pr, pi)
                    table[j, i, 32 * m + 16 : 32 * m + 24, :] = wr
                    table[j, i, 32 * m + 24 : 32 * m + 32, :] = wi
                for k in range(STEPS):
                    gr[j, i, 8 * k : 8 * k + 8, :] = gate[k] * y[k]
                    gm[j, i, 8 * k : 8 * k + 8, :] = gate[k] * m_first[k]

    def finish(j, copies):
        for copy in copies:
            copy.wait_recv()

        @pl.loop(0, width // 256)
        def _(i2):
            halves = []
            for h in range(2):
                i = 2 * i2 + h
                added = None
                for m in range(2):
                    r = 2 * i + m
                    ir = rows(inflow.at[j, i], m)
                    ii = rows(inflow.at[j, i], 2 + m)
                    a1 = rows(derived.at[j], 10 * n_rows + r)
                    a2 = rows(derived.at[j], 11 * n_rows + r)
                    t = [table[j, i, 32 * m + 8 * n : 32 * m + 8 * n + 8, :] for n in range(4)]
                    older = t[0] * ir - t[1] * ii
                    u = [t[2] * ir - t[3] * ii]
                    for k in range(1, STEPS):
                        u.append(a1 * u[-1] - a2 * older)
                        older = u[-2]
                    added = u if added is None else [a + b for a, b in zip(added, u)]
                halves.append(
                    jnp.concatenate(
                        [
                            gr[j, i, 8 * k : 8 * k + 8, :] + gm[j, i, 8 * k : 8 * k + 8, :] * added[k]
                            for k in range(STEPS)
                        ],
                        axis=0,
                    )
                )
            mixed = jnp.concatenate(halves, axis=1).astype(BF16)
            lane = pl.ds(pl.multiple_of(i2 * 256, 256), 256)
            obuf[j, :, lane] = jnp.dot(perm_out[...], mixed, preferred_element_type=F32).astype(BF16)

        columns = pl.ds(pl.multiple_of(block[j] * width, width), width)
        copy = pltpu.make_async_copy(obuf.at[j], out_hbm.at[0, :, columns], o_sem.at[j])
        copy.start()
        return copy

    one_copies = []
    for j in range(n_dp):
        if j:
            a_copies[j].wait_recv()
        h_copies[j].wait_recv()
        states(j)
        one_copies.append(gather_plane(j))
    two_copies = []
    for j in range(n_dp):
        two_copies.append(combine_plane(j, one_copies[j]))
        if j:
            b_copies[j].wait_recv()
        if j < n_dp - 1:
            response(j)
    response(n_dp - 1)
    three_copies = [combine_all(j, two_copies[j]) for j in range(n_dp)]
    stores = [finish(j, three_copies[j]) for j in range(n_dp)]
    for copy in sends:
        copy.wait_send()
    for copy in stores:
        copy.wait()


def local(n_dp, n_seq, streams, short_filter, decay_rate, pole_angle, residue_re, residue_im, skip_gain, doc_starts):
    width = short_filter.shape[2]
    plane = width // LANES
    n_z = n_seq // plane
    n_rows = 2 * plane
    vmem = pltpu.VMEM
    dma = pltpu.SemaphoreType.DMA
    anywhere = pl.BlockSpec(memory_space=pl.ANY)
    lines = TOK + 16
    return pl.pallas_call(
        functools.partial(kernel, n_dp, n_seq, plane),
        out_shape=jax.ShapeDtypeStruct((1, TOK, streams.shape[3]), BF16),
        in_specs=[anywhere] * 8,
        out_specs=anywhere,
        scratch_shapes=[
            vmem((n_dp, 3, TOK, width), BF16),
            vmem((n_dp, 16, width), BF16),
            vmem((n_dp, 16, width), BF16),
            vmem((3, 3, width), F32),
            vmem((2, width), F32),
            vmem((2, width), F32),
            vmem((2, width), F32),
            vmem((2, width), F32),
            vmem((1, width), F32),
            vmem((4, n_rows, LANES), F32),
            pltpu.SMEM(doc_starts.shape, jnp.int32),
            vmem((n_dp, 10 * plane, LANES), F32),
            vmem((n_dp, 8 * plane, LANES), F32),
            vmem((n_dp, 12 * n_rows, LANES), F32),
            vmem((3, lines, lines), BF16),
            vmem((TOK, TOK), BF16),
            vmem((STEPS, 8, LANES), F32),
            vmem((STEPS, 8, LANES), F32),
            vmem((STEPS, 8, LANES), F32),
            vmem((3, 8, LANES), F32),
            vmem((2, 8, LANES), F32),
            vmem((n_dp, plane, TOK, LANES), F32),
            vmem((n_dp, plane, TOK, LANES), F32),
            vmem((n_dp, plane, TOK, LANES), F32),
            vmem((n_dp, plane, 32, LANES), F32),
            vmem((n_dp, plane, 64, LANES), F32),
            vmem((n_dp, plane, 4, LANES), F32),
            vmem((n_dp, plane, 4, LANES), F32),
            vmem((n_dp, plane, 4, LANES), F32),
            vmem((n_dp, 4, LANES), F32),
            vmem((n_dp, n_z, 4, LANES), F32),
            vmem((n_dp, plane, 4, LANES), F32),
            vmem((n_dp, plane, 4, LANES), F32),
            vmem((n_dp, TOK, width), BF16),
            dma((7,)),
            dma((n_dp,)),
            dma((n_dp,)),
            dma((n_dp,)),
            dma((n_dp,)),
            dma((n_dp,)),
            dma((n_dp,)),
            dma((n_dp,)),
            dma((n_dp, plane - 1)),
            dma((n_dp, plane - 1)),
            dma((n_dp, n_z - 1)),
            dma((n_dp, n_z - 1)),
            dma((n_dp, plane - 1)),
            dma((n_dp, plane - 1)),
            dma((n_dp,)),
        ],
        compiler_params=pltpu.CompilerParams(collective_id=0, has_side_effects=True, vmem_limit_bytes=48 * 2**20),
        name="hyena_modal_scan",
    )(
        streams,
        short_filter,
        decay_rate,
        pole_angle,
        residue_re,
        residue_im,
        skip_gain.reshape(1, width),
        doc_starts,
    )


def solution(mesh):
    placed = (
        P(None, "dp", "seq", None),
        P(None, None, "dp"),
        P(None, "dp"),
        P(None, "dp"),
        P(None, "dp"),
        P(None, "dp"),
        P("dp"),
        P("dp", None),
    )
    return jax.shard_map(
        functools.partial(local, mesh.shape["dp"], mesh.shape["seq"]),
        mesh=mesh,
        in_specs=placed,
        out_specs=P("dp", "seq", None),
        check_vma=False,
    )
```

```python
import functools

import jax
import jax.numpy as jnp
from jax import lax
from jax.experimental import pallas as pl
from jax.experimental.pallas import tpu as pltpu
from jax.sharding import PartitionSpec as P

MESH = pl.DeviceIdType.MESH
F32 = jnp.float32
BF16 = jnp.bfloat16
LANES = 128
CHUNKS = 8
STEPS = 16
TOK = CHUNKS * STEPS


def iota(shape, axis):
    return lax.broadcasted_iota(jnp.int32, shape, axis)


def rows(ref, row, count=8):
    return jnp.broadcast_to(ref[pl.ds(row, 1), :], (count, LANES))


def cmul(ar, ai, br, bi):
    return ar * br - ai * bi, ar * bi + ai * br


def kernel(
    n_dp,
    n_seq,
    plane,
    streams_hbm,
    taps_hbm,
    decay_hbm,
    angle_hbm,
    resr_hbm,
    resi_hbm,
    skip_hbm,
    starts_hbm,
    out,
    xbuf,
    hsend,
    hrecv,
    xs,
    ends,
    obuf,
    taps_v,
    decay_v,
    angle_v,
    resr_v,
    resi_v,
    skip_v,
    raw,
    starts_s,
    par_a,
    par_b,
    derived,
    perm_in,
    perm_out,
    m_keep,
    m_tail,
    m_head,
    m_first,
    m_scan,
    m_dev,
    vbuf,
    gr,
    gm,
    excl,
    table,
    state,
    r1,
    pre,
    total,
    r2,
    back,
    inflow,
    in_sem,
    x_sem,
    pa_send,
    pa_recv,
    pb_send,
    pb_recv,
    h_send,
    h_recv,
    s1_send,
    s1_recv,
    s2_send,
    s2_recv,
    s3_send,
    s3_recv,
    o_sem,
    known,
):
    n_z = n_seq // plane
    width = plane * LANES
    me_x = lax.axis_index("dp")
    me = lax.axis_index("seq")
    me_z = me // plane
    me_q = me % plane
    offsets = [0]
    for d in range(1, n_dp // 2 + 1):
        offsets.append(d)
        if n_dp - d != d:
            offsets.append(n_dp - d)

    x_peer = [None] + [((me_x + n_dp - o) % n_dp, me) for o in offsets[1:]]
    q_rank = [(me_q + k) % plane for k in range(1, plane)]
    q_peer = [(me_x, me_z * plane + r) for r in q_rank]
    z_later = [(me_x, (me_z + k) % n_z * plane + me_q) for k in range(1, n_z)]
    after = (me_x, (me + 1) % n_seq)
    before = (me_x, (me + n_seq - 1) % n_seq)
    block = [(me_x + o) % n_dp for o in offsets]

    def z_at(shift):
        return (me_x, (me_z + shift + n_z) % n_z * plane + me_q)

    def either(shift):
        return [(me_z >= shift, z_at(-shift)), (me_z + shift < n_z, z_at(shift))]

    barrier = pltpu.get_barrier_semaphore()
    greeted = jnp.int32(0)
    for peer in x_peer[1:] + q_peer:
        pl.semaphore_signal(barrier, inc=1, device_id=peer, device_id_type=MESH)
        greeted += 1
    for near_by, peer in either(1) + [(me > 0, before), (me + 1 < n_seq, after)]:
        greeted += jnp.where(near_by, 1, 0)

        @pl.when(near_by)
        def _():
            pl.semaphore_signal(barrier, inc=1, device_id=peer, device_id_type=MESH)

    rounds = [d for d in (1, 2, 4, 8, 16) if d < n_z - 1]

    def tell(n):
        for there, peer in either(rounds[n]):

            @pl.when(there)
            def _():
                pl.semaphore_signal(known.at[n], inc=1, device_id=peer, device_id_type=MESH)

    def learn(n):
        count = jnp.int32(0)
        for there, _ in either(rounds[n]):
            count += jnp.where(there, 1, 0)
        pl.semaphore_wait(known.at[n], count)

    loads = [
        pltpu.make_async_copy(a, b, in_sem.at[n])
        for n, (a, b) in enumerate(
            [
                (taps_hbm, taps_v),
                (decay_hbm, decay_v),
                (angle_hbm, angle_v),
                (resr_hbm, resr_v),
                (resi_hbm, resi_v),
                (skip_hbm, skip_v),
                (starts_hbm, starts_s),
            ]
        )
    ]
    for copy in loads:
        copy.start()
    x_loads = []
    for j in range(n_dp):
        columns = pl.ds(pl.multiple_of(block[j] * width, width), width)
        copy = pltpu.make_async_copy(streams_hbm.at[:, 0, :, columns], xbuf.at[j], x_sem.at[j])
        copy.start()
        x_loads.append(copy)

    row = iota((TOK, TOK), 0)
    col = iota((TOK, TOK), 1)
    perm_in[...] = jnp.where(col == (row % CHUNKS) * STEPS + row // CHUNKS, 1.0, 0.0).astype(BF16)
    perm_out[...] = jnp.where(col == (row % STEPS) * CHUNKS + row // STEPS, 1.0, 0.0).astype(BF16)

    for copy in loads[:6]:
        copy.wait()
    for i in range(plane):
        lane = slice(i * LANES, (i + 1) * LANES)
        for s in range(2):
            for k in range(3):
                par_a[0, (3 * s + k) * plane + i, :] = taps_v[k, s, lane]
        for k in range(3):
            par_b[0, k * plane + i, :] = taps_v[k, 2, lane]
        par_b[0, 7 * plane + i, :] = skip_v[0, lane]
        for m in range(2):
            r = 2 * i + m
            for n, source in enumerate((decay_v, angle_v, resr_v, resi_v)):
                raw[n, r, :] = source[m, lane]
    decay = raw[0]
    magnitude = jnp.exp(-decay)
    par_a[0, 6 * plane : 8 * plane, :] = magnitude * jnp.cos(raw[1])
    par_a[0, 8 * plane : 10 * plane, :] = magnitude * jnp.sin(raw[1])
    square = decay * decay
    sinh = decay * (1.0 + square * (1.0 / 6.0) * (1.0 + square * (1.0 / 20.0) * (1.0 + square * (1.0 / 42.0))))
    norm = jnp.sqrt(2.0 * magnitude * sinh)
    par_b[0, 3 * plane : 5 * plane, :] = norm * raw[2]
    par_b[0, 5 * plane : 7 * plane, :] = norm * raw[3]

    @pl.when(me == 0)
    def _():
        hrecv[...] = jnp.zeros_like(hrecv)

    pl.semaphore_wait(barrier, greeted)

    def remote(source, target, send_sem, recv_sem, device):
        return pltpu.make_async_remote_copy(
            src_ref=source, dst_ref=target, send_sem=send_sem, recv_sem=recv_sem, device_id=device, device_id_type=MESH
        )

    def send_a(j):
        return remote(par_a.at[0], par_a.at[j], pa_send.at[j - 1], pa_recv.at[j - 1], x_peer[j])

    def send_b(j):
        return remote(par_b.at[0], par_b.at[j], pb_send.at[j - 1], pb_recv.at[j - 1], x_peer[j])

    def send_h(j):
        return remote(hsend.at[j], hrecv.at[j], h_send.at[j], h_recv.at[j], after)

    for j in range(1, n_dp):
        send_a(j).start()
    if rounds:
        tell(0)
    for j in range(n_dp):
        x_loads[j].wait()
        for s in range(3):
            hsend[j, 2 * s : 2 * s + 2, :] = xbuf[j, s, TOK - 16 :, :].astype(F32)[14:16]

        @pl.when(me + 1 < n_seq)
        def _():
            send_h(j).start()

    loads[6].wait()
    starts = [starts_s[0, d] for d in range(starts_s.shape[1])]
    near = [s - me * TOK for s in starts]
    chunk = iota((8, LANES), 0)
    one = jnp.ones((8, LANES), F32)
    zero = jnp.zeros((8, LANES), F32)

    def free(lo, hi, among):
        hit = (among[0] >= lo) & (among[0] < hi)
        for s in among[1:]:
            hit = hit | ((s >= lo) & (s < hi))
        return jnp.where(hit, zero, one)

    for k in range(STEPS):
        here = chunk * STEPS + k
        m_keep[k] = free(here, here + 1, near)
        tail = free(here + 1, chunk * STEPS + STEPS, near)
        if k < 2:
            m_head[k] = jnp.where(chunk == 0, tail, zero)
            tail = jnp.where(chunk == 0, zero, tail)
        m_tail[k] = tail
        m_first[k] = free(jnp.zeros_like(here), here + 1, near)
    for n, shift in enumerate((1, 2, 4)):
        reach = free((chunk - shift + 1) * STEPS, (chunk + 1) * STEPS, near)
        m_scan[n] = jnp.where(chunk >= shift, reach, zero)
    first_of_plane = me_z * plane * TOK
    m_dev[0] = free(first_of_plane + chunk * TOK, first_of_plane + (chunk + 1) * TOK, starts)
    m_dev[1] = free(chunk * plane * TOK, (chunk + 1) * plane * TOK, starts)

    has_before = jnp.where(me > 0, 1.0, 0.0).astype(F32)
    reach_near = 2 * rounds[1] if len(rounds) > 1 else n_z - 1
    near_planes = [k for k in range(1, n_z) if k <= reach_near]
    far_planes = [k for k in range(1, n_z) if k > reach_near]
    n_rows = 2 * plane
    log_plane = plane.bit_length() - 1

    def filters(j, i, source, base, x):
        c = [rows(source.at[j], (base + k) * plane + i) for k in range(3)]
        x = [pltpu.roll(x[STEPS - 2], 1, axis=0), pltpu.roll(x[STEPS - 1], 1, axis=0)] + x
        return [c[0] * x[k + 2] + c[1] * x[k + 1] + c[2] * x[k] for k in range(STEPS)]

    def first_two(j, s, i, source, base, x):
        c = [rows(source.at[j], (base + k) * plane + i) for k in range(3)]
        lane = pl.ds(pl.multiple_of(i * LANES, LANES), LANES)
        older = rows(hrecv.at[j, :, lane], 2 * s) * has_before
        old = rows(hrecv.at[j, :, lane], 2 * s + 1) * has_before
        return [c[0] * x[0] + c[1] * old + c[2] * older, c[0] * x[1] + c[1] * x[0] + c[2] * old]

    def permuted(j, s, i2):
        lane = pl.ds(pl.multiple_of(i2 * 256, 256), 256)
        return jnp.dot(perm_in[...], xbuf[j, s, :, lane], preferred_element_type=F32)

    def permute(j):
        for i2 in range(width // 256):
            for s in range(2):
                x = permuted(j, s, i2)
                xs[j, s, 2 * i2] = x[:, :LANES]
                xs[j, s, 2 * i2 + 1] = x[:, LANES:]

    def steps_of(ref, count=STEPS):
        return [ref[8 * k : 8 * k + 8, :] for k in range(count)]

    def powers(j):
        pr = par_a[j, 6 * plane : 8 * plane, :]
        pi = par_a[j, 8 * plane : 10 * plane, :]
        qr, qi = pr, pi
        tr, ti = pr, pi
        slot = 0
        for n in range(7 + log_plane):
            qr, qi = qr * qr - qi * qi, 2.0 * qr * qi
            if n == 0:
                tr, ti = qr, qi
            elif n < 3:
                tr, ti = cmul(tr, ti, qr, qi)
            if n + 1 in (4, 5, 6, 7, 7 + log_plane):
                derived[j, slot * n_rows : (slot + 1) * n_rows, :] = qr
                derived[j, (slot + 1) * n_rows : (slot + 2) * n_rows, :] = qi
                slot += 2
        derived[j, 10 * n_rows : 11 * n_rows, :] = 2.0 * pr
        derived[j, 11 * n_rows : 12 * n_rows, :] = pr * pr + pi * pi
        derived[j, 12 * n_rows : 13 * n_rows, :] = tr
        derived[j, 13 * n_rows : 14 * n_rows, :] = ti
        tr, ti = cmul(tr, ti, pr, pi)
        derived[j, 14 * n_rows : 15 * n_rows, :] = tr
        derived[j, 15 * n_rows : 16 * n_rows, :] = ti

    def products(j):
        powers(j)

        @pl.loop(0, plane // 2)
        def _(i2):
            for i in (2 * i2, 2 * i2 + 1):
                f0 = filters(j, i, par_a, 0, steps_of(xs.at[j, 0, i]))
                f1 = filters(j, i, par_a, 3, steps_of(xs.at[j, 1, i]))
                masked = []
                for k in range(STEPS):
                    v = f0[k] * f1[k]
                    vbuf[j, i, 8 * k : 8 * k + 8, :] = v
                    masked.append(v * m_tail[k])
                for m in range(2):
                    r = 2 * i + m
                    a1 = rows(derived.at[j], 10 * n_rows + r)
                    a2 = rows(derived.at[j], 11 * n_rows + r)
                    b2, b1 = masked[0], a1 * masked[0] + masked[1]
                    for k in range(2, STEPS):
                        b1, b2 = a1 * b1 + (masked[k] - a2 * b2), b1
                    ends[j, i, 16 * m : 16 * m + 8, :] = b1 - rows(par_a.at[j], 6 * plane + r) * b2
                    ends[j, i, 16 * m + 8 : 16 * m + 16, :] = rows(par_a.at[j], 8 * plane + r) * b2

    def states(j):
        @pl.loop(0, plane // 2)
        def _(i2):
            for i in (2 * i2, 2 * i2 + 1):
                f0 = first_two(j, 0, i, par_a, 0, steps_of(xs.at[j, 0, i], 2))
                f1 = first_two(j, 1, i, par_a, 3, steps_of(xs.at[j, 1, i], 2))
                v = [f0[k] * f1[k] for k in range(2)]
                for k in range(2):
                    vbuf[j, i, 8 * k : 8 * k + 8, :] = jnp.where(
                        chunk == 0, v[k], vbuf[j, i, 8 * k : 8 * k + 8, :]
                    )
                v = [v[k] * m_head[k] for k in range(2)]
                for m in range(2):
                    r = 2 * i + m
                    p14, q14, p15, q15 = [rows(derived.at[j], (12 + n) * n_rows + r) for n in range(4)]
                    er = ends[j, i, 16 * m : 16 * m + 8, :] + (v[0] * p15 + v[1] * p14)
                    ei = ends[j, i, 16 * m + 8 : 16 * m + 16, :] + (v[0] * q15 + v[1] * q14)
                    for n, shift in enumerate((1, 2, 4)):
                        reach = m_scan[n]
                        kr = reach * rows(derived.at[j], 2 * n * n_rows + r)
                        ki = reach * rows(derived.at[j], (2 * n + 1) * n_rows + r)
                        sr = pltpu.roll(er, shift, axis=0)
                        si = pltpu.roll(ei, shift, axis=0)
                        ar, ai = cmul(kr, ki, sr, si)
                        er, ei = er + ar, ei + ai
                    state[j, i, pl.ds(m, 1), :] = er[7:8]
                    state[j, i, pl.ds(2 + m, 1), :] = ei[7:8]
                    later = jnp.where(chunk >= 1, one, zero)
                    excl[j, i, 16 * m : 16 * m + 8, :] = pltpu.roll(er, 1, axis=0) * later
                    excl[j, i, 16 * m + 8 : 16 * m + 16, :] = pltpu.roll(ei, 1, axis=0) * later

    def gather_plane(j):
        r1[j, me_q] = state[j, me_q]
        for n in range(plane - 1):
            remote(state.at[j, q_rank[n]], r1.at[j, me_q], s1_send.at[j], s1_recv.at[j], q_peer[n]).start()

    def whole_1(j):
        others = pl.ds(0, plane - 1)
        return remote(state.at[j, others], r1.at[j, others], s1_send.at[j], s1_recv.at[j], q_peer[0])

    def whole_3(j):
        others = pl.ds(0, plane - 1)
        return remote(back.at[j, others], inflow.at[j, others], s3_send.at[j], s3_recv.at[j], q_peer[0])

    def send_2(j, k):
        return remote(total.at[j], r2.at[j, me_z], s2_send.at[j, k - 1], s2_recv.at[j, k - 1], z_later[k - 1])

    def later_planes(j, distances, act):
        for k in distances:

            @pl.when(me_z + k < n_z)
            def _():
                act(send_2(j, k))

    def combine_plane(j):
        whole_1(j).wait_recv()
        pr = derived[j, pl.ds(6 * n_rows + 2 * me_q, 2), :]
        pi = derived[j, pl.ds(7 * n_rows + 2 * me_q, 2), :]
        run_r = jnp.zeros((2, LANES), F32)
        run_i = run_r
        for e in range(plane):
            pre[j, e, 0:2, :] = run_r
            pre[j, e, 2:4, :] = run_i
            keep = m_dev[0, e : e + 1, :]
            ar, ai = cmul(pr * keep, pi * keep, run_r, run_i)
            run_r = ar + r1[j, e, 0:2, :]
            run_i = ai + r1[j, e, 2:4, :]
        total[j, 0:2, :] = run_r
        total[j, 2:4, :] = run_i
        later_planes(j, near_planes, lambda copy: copy.start())

    def combine_all(j):
        for k in range(1, n_z):

            @pl.when(me_z >= k)
            def _():
                send_2(j, k).wait_recv()

        pr = derived[j, pl.ds(8 * n_rows + 2 * me_q, 2), :]
        pi = derived[j, pl.ds(9 * n_rows + 2 * me_q, 2), :]
        run_r = jnp.zeros((2, LANES), F32)
        run_i = run_r
        for z in range(n_z - 1):
            keep = m_dev[1, z : z + 1, :]
            ar, ai = cmul(pr * keep, pi * keep, run_r, run_i)
            past = z < me_z
            run_r = jnp.where(past, ar + r2[j, z, 0:2, :], run_r)
            run_i = jnp.where(past, ai + r2[j, z, 2:4, :], run_i)
        pr = derived[j, pl.ds(6 * n_rows + 2 * me_q, 2), :]
        pi = derived[j, pl.ds(7 * n_rows + 2 * me_q, 2), :]
        for e in range(plane):
            back[j, e, 0:2, :] = pre[j, e, 0:2, :] + run_r
            back[j, e, 2:4, :] = pre[j, e, 2:4, :] + run_i
            keep = m_dev[0, e : e + 1, :]
            run_r, run_i = cmul(pr * keep, pi * keep, run_r, run_i)
        inflow[j, me_q] = back[j, me_q]
        for n in range(plane - 1):
            remote(back.at[j, q_rank[n]], inflow.at[j, me_q], s3_send.at[j], s3_recv.at[j], q_peer[n]).start()

    def response(j):
        @pl.loop(0, width // 256)
        def _(i2):
            x2 = permuted(j, 2, i2)
            for h in range(2):
                i = 2 * i2 + h
                x = [x2[8 * k : 8 * k + 8, h * LANES : (h + 1) * LANES] for k in range(STEPS)]
                gate = filters(j, i, par_b, 0, x)
                head = first_two(j, 2, i, par_b, 0, x)
                for k in range(2):
                    gate[k] = jnp.where(chunk == 0, head[k], gate[k])
                skip = rows(par_b.at[j], 7 * plane + i)
                v = [vbuf[j, i, 8 * k : 8 * k + 8, :] for k in range(STEPS)]
                y = [skip * v[k] for k in range(STEPS)]
                for m in range(2):
                    r = 2 * i + m
                    pr = rows(par_a.at[j], 6 * plane + r)
                    pi = rows(par_a.at[j], 8 * plane + r)
                    wr = rows(par_b.at[j], 3 * plane + r)
                    wi = rows(par_b.at[j], 5 * plane + r)
                    sr = excl[j, i, 16 * m : 16 * m + 8, :]
                    si = excl[j, i, 16 * m + 8 : 16 * m + 16, :]
                    for k in range(STEPS):
                        keep = m_keep[k]
                        tr, ti = keep * sr, keep * si
                        sr = pr * tr - pi * ti + v[k]
                        si = pr * ti + pi * tr
                        y[k] = y[k] + (wr * sr - wi * si)
                    for n, bit in enumerate((1, 2, 4)):
                        on = (chunk & bit) > 0
                        br = jnp.where(on, rows(derived.at[j], 2 * n * n_rows + r), one)
                        bi = jnp.where(on, rows(derived.at[j], (2 * n + 1) * n_rows + r), zero)
                        wr, wi = cmul(wr, wi, br, bi)
                    table[j, i, 32 * m : 32 * m + 8, :] = wr
                    table[j, i, 32 * m + 8 : 32 * m + 16, :] = wi
                    wr, wi = cmul(wr, wi, pr, pi)
                    table[j, i, 32 * m + 16 : 32 * m + 24, :] = wr
                    table[j, i, 32 * m + 24 : 32 * m + 32, :] = wi
                for k in range(STEPS):
                    gr[j, i, 8 * k : 8 * k + 8, :] = gate[k] * y[k]
                    gm[j, i, 8 * k : 8 * k + 8, :] = gate[k] * m_first[k]

    def finish(j):
        whole_3(j).wait_recv()

        for i2 in range(width // 256):
            halves = []
            for h in range(2):
                i = 2 * i2 + h
                added = None
                for m in range(2):
                    r = 2 * i + m
                    ir = rows(inflow.at[j, i], m)
                    ii = rows(inflow.at[j, i], 2 + m)
                    a1 = rows(derived.at[j], 10 * n_rows + r)
                    a2 = rows(derived.at[j], 11 * n_rows + r)
                    t = [table[j, i, 32 * m + 8 * n : 32 * m + 8 * n + 8, :] for n in range(4)]
                    older = t[0] * ir - t[1] * ii
                    u = [t[2] * ir - t[3] * ii]
                    for k in range(1, STEPS):
                        u.append(a1 * u[-1] - a2 * older)
                        older = u[-2]
                    added = u if added is None else [a + b for a, b in zip(added, u)]
                halves.append(
                    jnp.concatenate(
                        [
                            gr[j, i, 8 * k : 8 * k + 8, :] + gm[j, i, 8 * k : 8 * k + 8, :] * added[k]
                            for k in range(STEPS)
                        ],
                        axis=0,
                    )
                )
            mixed = jnp.concatenate(halves, axis=1).astype(BF16)
            obuf[j, :, i2 * 256 : i2 * 256 + 256] = jnp.dot(perm_out[...], mixed, preferred_element_type=F32).astype(BF16)
        columns = pl.ds(pl.multiple_of(block[j] * width, width), width)
        copy = pltpu.make_async_copy(obuf.at[j], out.at[0, :, columns], o_sem.at[j])
        copy.start()
        return copy

    for j in range(n_dp):
        permute(j)
    products(0)
    if rounds:
        learn(0)
    if len(rounds) > 1:
        tell(1)
    for j in range(1, n_dp):
        send_a(j).wait_recv()
        products(j)
    for j in range(1, n_dp):
        send_b(j).start()
    for j in range(n_dp):

        @pl.when(me > 0)
        def _():
            send_h(j).wait_recv()

        states(j)
        gather_plane(j)
    if len(rounds) > 1:
        learn(1)
    if len(rounds) > 2:
        tell(2)
    response(0)
    for j in range(n_dp):
        combine_plane(j)
    for j in range(1, n_dp):
        send_b(j).wait_recv()
        response(j)
    for j in range(n_dp):
        combine_all(j)
    if far_planes:
        learn(2)
    for j in range(n_dp):
        later_planes(j, far_planes, lambda copy: copy.start())
    stores = [finish(j) for j in range(n_dp)]
    for j in range(n_dp):
        if j:
            send_a(j).wait_send()
            send_b(j).wait_send()

        @pl.when(me + 1 < n_seq)
        def _():
            send_h(j).wait_send()

        whole_1(j).wait_send()
        later_planes(j, range(1, n_z), lambda copy: copy.wait_send())
        whole_3(j).wait_send()
    for copy in stores:
        copy.wait()


def local(n_dp, n_seq, streams, short_filter, decay_rate, pole_angle, residue_re, residue_im, skip_gain, doc_starts):
    width = short_filter.shape[2]
    plane = width // LANES
    n_z = n_seq // plane
    n_rows = 2 * plane
    vmem = pltpu.VMEM
    dma = pltpu.SemaphoreType.DMA
    anywhere = pl.BlockSpec(memory_space=pl.ANY)
    return pl.pallas_call(
        functools.partial(kernel, n_dp, n_seq, plane),
        out_shape=jax.ShapeDtypeStruct((1, TOK, streams.shape[3]), BF16),
        in_specs=[anywhere] * 8,
        out_specs=anywhere,
        scratch_shapes=[
            vmem((n_dp, 3, TOK, width), BF16),
            vmem((n_dp, 8, width), F32),
            vmem((n_dp, 8, width), F32),
            vmem((n_dp, 2, plane, TOK, LANES), F32),
            vmem((n_dp, plane, 32, LANES), F32),
            vmem((n_dp, TOK, width), BF16),
            vmem((3, 3, width), F32),
            vmem((2, width), F32),
            vmem((2, width), F32),
            vmem((2, width), F32),
            vmem((2, width), F32),
            vmem((1, width), F32),
            vmem((4, n_rows, LANES), F32),
            pltpu.SMEM(doc_starts.shape, jnp.int32),
            vmem((n_dp, 10 * plane, LANES), F32),
            vmem((n_dp, 8 * plane, LANES), F32),
            vmem((n_dp, 16 * n_rows, LANES), F32),
            vmem((TOK, TOK), BF16),
            vmem((TOK, TOK), BF16),
            vmem((STEPS, 8, LANES), F32),
            vmem((STEPS, 8, LANES), F32),
            vmem((2, 8, LANES), F32),
            vmem((STEPS, 8, LANES), F32),
            vmem((3, 8, LANES), F32),
            vmem((2, 8, LANES), F32),
            vmem((n_dp, plane, TOK, LANES), F32),
            vmem((n_dp, plane, TOK, LANES), F32),
            vmem((n_dp, plane, TOK, LANES), F32),
            vmem((n_dp, plane, 32, LANES), F32),
            vmem((n_dp, plane, 64, LANES), F32),
            vmem((n_dp, plane, 4, LANES), F32),
            vmem((n_dp, plane, 4, LANES), F32),
            vmem((n_dp, plane, 4, LANES), F32),
            vmem((n_dp, 4, LANES), F32),
            vmem((n_dp, n_z, 4, LANES), F32),
            vmem((n_dp, plane, 4, LANES), F32),
            vmem((n_dp, plane, 4, LANES), F32),
            dma((7,)),
            dma((n_dp,)),
            dma((n_dp - 1,)),
            dma((n_dp - 1,)),
            dma((n_dp - 1,)),
            dma((n_dp - 1,)),
            dma((n_dp,)),
            dma((n_dp,)),
            dma((n_dp,)),
            dma((n_dp,)),
            dma((n_dp, n_z - 1)),
            dma((n_dp, n_z - 1)),
            dma((n_dp,)),
            dma((n_dp,)),
            dma((n_dp,)),
            pltpu.SemaphoreType.REGULAR((3,)),
        ],
        compiler_params=pltpu.CompilerParams(collective_id=0, has_side_effects=True, vmem_limit_bytes=48 * 2**20),
        name="hyena_modal_scan",
    )(
        *[
            pltpu.with_memory_space_constraint(a, pltpu.HBM)
            for a in (
                streams,
                short_filter,
                decay_rate,
                pole_angle,
                residue_re,
                residue_im,
                skip_gain.reshape(1, width),
                doc_starts,
            )
        ]
    )


def solution(mesh):
    placed = (
        P(None, "dp", "seq", None),
        P(None, None, "dp"),
        P(None, "dp"),
        P(None, "dp"),
        P(None, "dp"),
        P(None, "dp"),
        P("dp"),
        P("dp", None),
    )
    return jax.shard_map(
        functools.partial(local, mesh.shape["dp"], mesh.shape["seq"]),
        mesh=mesh,
        in_specs=placed,
        out_specs=P("dp", "seq", None),
        check_vma=False,
    )
```

```python
import functools

import jax
import jax.numpy as jnp
from jax import lax
from jax.experimental import pallas as pl
from jax.experimental.pallas import tpu as pltpu
from jax.sharding import PartitionSpec as P

MESH = pl.DeviceIdType.MESH
F32 = jnp.float32
BF16 = jnp.bfloat16
LANES = 128
CHUNKS = 8
STEPS = 16
TOK = CHUNKS * STEPS


def iota(shape, axis):
    return lax.broadcasted_iota(jnp.int32, shape, axis)


def rows(ref, row, count=8):
    return jnp.broadcast_to(ref[pl.ds(row, 1), :], (count, LANES))


def cmul(ar, ai, br, bi):
    return ar * br - ai * bi, ar * bi + ai * br


def kernel(
    n_dp,
    n_seq,
    plane,
    streams_hbm,
    taps_hbm,
    decay_hbm,
    angle_hbm,
    resr_hbm,
    resi_hbm,
    skip_hbm,
    starts_hbm,
    out,
    xbuf,
    hsend,
    hrecv,
    hsrc,
    hrows,
    xs,
    ends,
    obuf,
    taps_v,
    decay_v,
    angle_v,
    resr_v,
    resi_v,
    skip_v,
    raw,
    starts_s,
    par_a,
    par_b,
    derived,
    perm_in,
    perm_out,
    m_keep,
    m_tail,
    m_head,
    m_first,
    m_scan,
    m_dev,
    vbuf,
    gr,
    gm,
    excl,
    table,
    state,
    r1,
    pre,
    total,
    r2,
    back,
    inflow,
    in_sem,
    x_sem,
    pa_send,
    pa_recv,
    pb_send,
    pb_recv,
    h_send,
    h_recv,
    s1_send,
    s1_recv,
    s2_send,
    s2_recv,
    s3_send,
    s3_recv,
    o_sem,
    known,
):
    n_z = n_seq // plane
    width = plane * LANES
    me_x = lax.axis_index("dp")
    me = lax.axis_index("seq")
    me_z = me // plane
    me_q = me % plane
    offsets = [0]
    for d in range(1, n_dp // 2 + 1):
        offsets.append(d)
        if n_dp - d != d:
            offsets.append(n_dp - d)

    x_peer = [None] + [((me_x + n_dp - o) % n_dp, me) for o in offsets[1:]]
    q_rank = [(me_q + k) % plane for k in range(1, plane)]
    q_peer = [(me_x, me_z * plane + r) for r in q_rank]
    z_later = [(me_x, (me_z + k) % n_z * plane + me_q) for k in range(1, n_z)]
    after = (me_x, (me + 1) % n_seq)
    before = (me_x, (me + n_seq - 1) % n_seq)
    block = [(me_x + o) % n_dp for o in offsets]

    def z_at(shift):
        return (me_x, (me_z + shift + n_z) % n_z * plane + me_q)

    def either(shift):
        return [(me_z >= shift, z_at(-shift)), (me_z + shift < n_z, z_at(shift))]

    barrier = pltpu.get_barrier_semaphore()
    greeted = jnp.int32(0)
    for peer in x_peer[1:] + q_peer:
        pl.semaphore_signal(barrier, inc=1, device_id=peer, device_id_type=MESH)
        greeted += 1
    for near_by, peer in either(1) + [(me > 0, before), (me + 1 < n_seq, after)]:
        greeted += jnp.where(near_by, 1, 0)

        @pl.when(near_by)
        def _():
            pl.semaphore_signal(barrier, inc=1, device_id=peer, device_id_type=MESH)

    rounds = [d for d in (1, 2, 4, 8, 16) if d < n_z - 1]

    def tell(n):
        for there, peer in either(rounds[n]):

            @pl.when(there)
            def _():
                pl.semaphore_signal(known.at[n], inc=1, device_id=peer, device_id_type=MESH)

    def learn(n):
        count = jnp.int32(0)
        for there, _ in either(rounds[n]):
            count += jnp.where(there, 1, 0)
        pl.semaphore_wait(known.at[n], count)

    loads = [
        pltpu.make_async_copy(a, b, in_sem.at[n])
        for n, (a, b) in enumerate(
            [
                (taps_hbm, taps_v),
                (decay_hbm, decay_v),
                (angle_hbm, angle_v),
                (resr_hbm, resr_v),
                (resi_hbm, resi_v),
                (skip_hbm, skip_v),
                (starts_hbm, starts_s),
            ]
        )
    ]
    for copy in loads:
        copy.start()
    x_load = pltpu.make_async_copy(streams_hbm.at[:, 0], xbuf, x_sem)
    x_load.start()

    row = iota((TOK, TOK), 0)
    col = iota((TOK, TOK), 1)
    perm_in[...] = jnp.where(col == (row % CHUNKS) * STEPS + row // CHUNKS, 1.0, 0.0).astype(BF16)
    perm_out[...] = jnp.where(col == (row % STEPS) * CHUNKS + row // STEPS, 1.0, 0.0).astype(BF16)

    for copy in loads[:6]:
        copy.wait()
    for i in range(plane):
        lane = slice(i * LANES, (i + 1) * LANES)
        for s in range(2):
            for k in range(3):
                par_a[0, (3 * s + k) * plane + i, :] = taps_v[k, s, lane]
        for k in range(3):
            par_b[0, k * plane + i, :] = taps_v[k, 2, lane]
        par_b[0, 7 * plane + i, :] = skip_v[0, lane]
        for m in range(2):
            r = 2 * i + m
            for n, source in enumerate((decay_v, angle_v, resr_v, resi_v)):
                raw[n, r, :] = source[m, lane]
    decay = raw[0]
    magnitude = jnp.exp(-decay)
    par_a[0, 6 * plane : 8 * plane, :] = magnitude * jnp.cos(raw[1])
    par_a[0, 8 * plane : 10 * plane, :] = magnitude * jnp.sin(raw[1])
    square = decay * decay
    sinh = decay * (1.0 + square * (1.0 / 6.0) * (1.0 + square * (1.0 / 20.0) * (1.0 + square * (1.0 / 42.0))))
    norm = jnp.sqrt(2.0 * magnitude * sinh)
    par_b[0, 3 * plane : 5 * plane, :] = norm * raw[2]
    par_b[0, 5 * plane : 7 * plane, :] = norm * raw[3]

    @pl.when(me == 0)
    def _():
        hrecv[...] = jnp.zeros_like(hrecv)

    hsrc[...] = jnp.zeros_like(hsrc)

    pl.semaphore_wait(barrier, greeted)

    def remote(source, target, send_sem, recv_sem, device):
        return pltpu.make_async_remote_copy(
            src_ref=source, dst_ref=target, send_sem=send_sem, recv_sem=recv_sem, device_id=device, device_id_type=MESH
        )

    def send_a(j):
        return remote(par_a.at[0], par_a.at[j], pa_send.at[j - 1], pa_recv.at[j - 1], x_peer[j])

    def send_b(j):
        return remote(par_b.at[0], par_b.at[j], pb_send.at[j - 1], pb_recv.at[j - 1], x_peer[j])

    for j in range(1, n_dp):
        send_a(j).start()
    if rounds:
        tell(0)
    x_load.wait()
    half = n_dp * width // 2
    for s in range(3):
        last = xbuf[s, TOK - 16 :, :].astype(F32)[14:16]
        for h in range(2):
            hsrc[8 * h + 2 * s : 8 * h + 2 * s + 2, :] = last[:, h * half : (h + 1) * half]
    hsend[...] = hsrc[...].astype(BF16)

    def send_h():
        return remote(hsend, hrecv, h_send, h_recv, after)

    @pl.when(me + 1 < n_seq)
    def _():
        send_h().start()

    loads[6].wait()
    starts = [starts_s[0, d] for d in range(starts_s.shape[1])]
    near = [s - me * TOK for s in starts]
    chunk = iota((8, LANES), 0)
    one = jnp.ones((8, LANES), F32)
    zero = jnp.zeros((8, LANES), F32)

    def free(lo, hi, among):
        hit = (among[0] >= lo) & (among[0] < hi)
        for s in among[1:]:
            hit = hit | ((s >= lo) & (s < hi))
        return jnp.where(hit, zero, one)

    for k in range(STEPS):
        here = chunk * STEPS + k
        m_keep[k] = free(here, here + 1, near)
        tail = free(here + 1, chunk * STEPS + STEPS, near)
        if k < 2:
            m_head[k] = jnp.where(chunk == 0, tail, zero)
            tail = jnp.where(chunk == 0, zero, tail)
        m_tail[k] = tail
        m_first[k] = free(jnp.zeros_like(here), here + 1, near)
    for n, shift in enumerate((1, 2, 4)):
        reach = free((chunk - shift + 1) * STEPS, (chunk + 1) * STEPS, near)
        m_scan[n] = jnp.where(chunk >= shift, reach, zero)
    first_of_plane = me_z * plane * TOK
    m_dev[0] = free(first_of_plane + chunk * TOK, first_of_plane + (chunk + 1) * TOK, starts)
    m_dev[1] = free(chunk * plane * TOK, (chunk + 1) * plane * TOK, starts)

    reach_near = 2 * rounds[1] if len(rounds) > 1 else n_z - 1
    near_planes = [k for k in range(1, n_z) if k <= reach_near]
    far_planes = [k for k in range(1, n_z) if k > reach_near]
    n_rows = 2 * plane
    log_plane = plane.bit_length() - 1

    def filters(j, i, source, base, x):
        c = [rows(source.at[j], (base + k) * plane + i) for k in range(3)]
        x = [pltpu.roll(x[STEPS - 2], 1, axis=0), pltpu.roll(x[STEPS - 1], 1, axis=0)] + x
        return [c[0] * x[k + 2] + c[1] * x[k + 1] + c[2] * x[k] for k in range(STEPS)]

    def first_two(j, s, i, source, base, x):
        c = [rows(source.at[j], (base + k) * plane + i) for k in range(3)]
        older = rows(hrows.at[block[j] * plane + i], 2 * s)
        old = rows(hrows.at[block[j] * plane + i], 2 * s + 1)
        return [c[0] * x[0] + c[1] * old + c[2] * older, c[0] * x[1] + c[1] * x[0] + c[2] * old]

    def permuted(j, s, i2):
        lane = pl.ds(pl.multiple_of(block[j] * width + i2 * 256, 256), 256)
        return jnp.dot(perm_in[...], xbuf[s, :, lane], preferred_element_type=F32)

    def permute(j):
        for i2 in range(width // 256):
            for s in range(2):
                x = permuted(j, s, i2)
                xs[j, s, 2 * i2] = x[:, :LANES]
                xs[j, s, 2 * i2 + 1] = x[:, LANES:]

    def steps_of(ref, count=STEPS):
        return [ref[8 * k : 8 * k + 8, :] for k in range(count)]

    def powers(j):
        pr = par_a[j, 6 * plane : 8 * plane, :]
        pi = par_a[j, 8 * plane : 10 * plane, :]
        qr, qi = pr, pi
        tr, ti = pr, pi
        slot = 0
        for n in range(7 + log_plane):
            qr, qi = qr * qr - qi * qi, 2.0 * qr * qi
            if n == 0:
                tr, ti = qr, qi
            elif n < 3:
                tr, ti = cmul(tr, ti, qr, qi)
            if n + 1 in (4, 5, 6, 7, 7 + log_plane):
                derived[j, slot * n_rows : (slot + 1) * n_rows, :] = qr
                derived[j, (slot + 1) * n_rows : (slot + 2) * n_rows, :] = qi
                slot += 2
        derived[j, 10 * n_rows : 11 * n_rows, :] = 2.0 * pr
        derived[j, 11 * n_rows : 12 * n_rows, :] = pr * pr + pi * pi
        derived[j, 12 * n_rows : 13 * n_rows, :] = tr
        derived[j, 13 * n_rows : 14 * n_rows, :] = ti
        tr, ti = cmul(tr, ti, pr, pi)
        derived[j, 14 * n_rows : 15 * n_rows, :] = tr
        derived[j, 15 * n_rows : 16 * n_rows, :] = ti

    def products(j):
        powers(j)

        @pl.loop(0, plane // 2)
        def _(i2):
            for i in (2 * i2, 2 * i2 + 1):
                f0 = filters(j, i, par_a, 0, steps_of(xs.at[j, 0, i]))
                f1 = filters(j, i, par_a, 3, steps_of(xs.at[j, 1, i]))
                masked = []
                for k in range(STEPS):
                    v = f0[k] * f1[k]
                    vbuf[j, i, 8 * k : 8 * k + 8, :] = v
                    masked.append(v * m_tail[k])
                for m in range(2):
                    r = 2 * i + m
                    a1 = rows(derived.at[j], 10 * n_rows + r)
                    a2 = rows(derived.at[j], 11 * n_rows + r)
                    b2, b1 = masked[0], a1 * masked[0] + masked[1]
                    for k in range(2, STEPS):
                        b1, b2 = a1 * b1 + (masked[k] - a2 * b2), b1
                    ends[j, i, 16 * m : 16 * m + 8, :] = b1 - rows(par_a.at[j], 6 * plane + r) * b2
                    ends[j, i, 16 * m + 8 : 16 * m + 16, :] = rows(par_a.at[j], 8 * plane + r) * b2

    def states(j):
        @pl.loop(0, plane // 2)
        def _(i2):
            for i in (2 * i2, 2 * i2 + 1):
                f0 = first_two(j, 0, i, par_a, 0, steps_of(xs.at[j, 0, i], 2))
                f1 = first_two(j, 1, i, par_a, 3, steps_of(xs.at[j, 1, i], 2))
                v = [f0[k] * f1[k] for k in range(2)]
                for k in range(2):
                    vbuf[j, i, 8 * k : 8 * k + 8, :] = jnp.where(
                        chunk == 0, v[k], vbuf[j, i, 8 * k : 8 * k + 8, :]
                    )
                v = [v[k] * m_head[k] for k in range(2)]
                for m in range(2):
                    r = 2 * i + m
                    p14, q14, p15, q15 = [rows(derived.at[j], (12 + n) * n_rows + r) for n in range(4)]
                    er = ends[j, i, 16 * m : 16 * m + 8, :] + (v[0] * p15 + v[1] * p14)
                    ei = ends[j, i, 16 * m + 8 : 16 * m + 16, :] + (v[0] * q15 + v[1] * q14)
                    for n, shift in enumerate((1, 2, 4)):
                        reach = m_scan[n]
                        kr = reach * rows(derived.at[j], 2 * n * n_rows + r)
                        ki = reach * rows(derived.at[j], (2 * n + 1) * n_rows + r)
                        sr = pltpu.roll(er, shift, axis=0)
                        si = pltpu.roll(ei, shift, axis=0)
                        ar, ai = cmul(kr, ki, sr, si)
                        er, ei = er + ar, ei + ai
                    state[j, i, pl.ds(m, 1), :] = er[7:8]
                    state[j, i, pl.ds(2 + m, 1), :] = ei[7:8]
                    later = jnp.where(chunk >= 1, one, zero)
                    excl[j, i, 16 * m : 16 * m + 8, :] = pltpu.roll(er, 1, axis=0) * later
                    excl[j, i, 16 * m + 8 : 16 * m + 16, :] = pltpu.roll(ei, 1, axis=0) * later

    def gather_plane(j):
        r1[j, me_q] = state[j, me_q]
        for n in range(plane - 1):
            remote(state.at[j, q_rank[n]], r1.at[j, me_q], s1_send.at[j], s1_recv.at[j], q_peer[n]).start()

    def whole_1(j):
        others = pl.ds(0, plane - 1)
        return remote(state.at[j, others], r1.at[j, others], s1_send.at[j], s1_recv.at[j], q_peer[0])

    def whole_3(j):
        others = pl.ds(0, plane - 1)
        return remote(back.at[j, others], inflow.at[j, others], s3_send.at[j], s3_recv.at[j], q_peer[0])

    def send_2(j, k):
        return remote(total.at[j], r2.at[j, me_z], s2_send.at[j], s2_recv.at[j], z_later[k - 1])

    def later_planes(j, distances):
        for k in distances:

            @pl.when(me_z + k < n_z)
            def _():
                send_2(j, k).start()

    def whole_2(j, count):
        those = pl.ds(0, count)
        return remote(r2.at[j, those], r2.at[j, those], s2_send.at[j], s2_recv.at[j], z_later[0])

    def combine_plane(j):
        whole_1(j).wait_recv()
        pr = derived[j, pl.ds(6 * n_rows + 2 * me_q, 2), :]
        pi = derived[j, pl.ds(7 * n_rows + 2 * me_q, 2), :]
        run_r = jnp.zeros((2, LANES), F32)
        run_i = run_r
        for e in range(plane):
            pre[j, e, 0:2, :] = run_r
            pre[j, e, 2:4, :] = run_i
            keep = m_dev[0, e : e + 1, :]
            ar, ai = cmul(pr * keep, pi * keep, run_r, run_i)
            run_r = ar + r1[j, e, 0:2, :]
            run_i = ai + r1[j, e, 2:4, :]
        total[j, 0:2, :] = run_r
        total[j, 2:4, :] = run_i
        later_planes(j, near_planes)

    def combine_all(j):
        for count in range(1, n_z):

            @pl.when(me_z == count)
            def _():
                whole_2(j, count).wait_recv()

        pr = derived[j, pl.ds(8 * n_rows + 2 * me_q, 2), :]
        pi = derived[j, pl.ds(9 * n_rows + 2 * me_q, 2), :]
        run_r = jnp.zeros((2, LANES), F32)
        run_i = run_r
        for z in range(n_z - 1):
            keep = m_dev[1, z : z + 1, :]
            ar, ai = cmul(pr * keep, pi * keep, run_r, run_i)
            past = z < me_z
            run_r = jnp.where(past, ar + r2[j, z, 0:2, :], run_r)
            run_i = jnp.where(past, ai + r2[j, z, 2:4, :], run_i)
        pr = derived[j, pl.ds(6 * n_rows + 2 * me_q, 2), :]
        pi = derived[j, pl.ds(7 * n_rows + 2 * me_q, 2), :]
        for e in range(plane):
            back[j, e, 0:2, :] = pre[j, e, 0:2, :] + run_r
            back[j, e, 2:4, :] = pre[j, e, 2:4, :] + run_i
            keep = m_dev[0, e : e + 1, :]
            run_r, run_i = cmul(pr * keep, pi * keep, run_r, run_i)
        inflow[j, me_q] = back[j, me_q]
        for n in range(plane - 1):
            remote(back.at[j, q_rank[n]], inflow.at[j, me_q], s3_send.at[j], s3_recv.at[j], q_peer[n]).start()

    def response(j):
        @pl.loop(0, width // 256)
        def _(i2):
            x2 = permuted(j, 2, i2)
            for h in range(2):
                i = 2 * i2 + h
                x = [x2[8 * k : 8 * k + 8, h * LANES : (h + 1) * LANES] for k in range(STEPS)]
                gate = filters(j, i, par_b, 0, x)
                head = first_two(j, 2, i, par_b, 0, x)
                for k in range(2):
                    gate[k] = jnp.where(chunk == 0, head[k], gate[k])
                skip = rows(par_b.at[j], 7 * plane + i)
                v = [vbuf[j, i, 8 * k : 8 * k + 8, :] for k in range(STEPS)]
                y = [skip * v[k] for k in range(STEPS)]
                for m in range(2):
                    r = 2 * i + m
                    pr = rows(par_a.at[j], 6 * plane + r)
                    pi = rows(par_a.at[j], 8 * plane + r)
                    wr = rows(par_b.at[j], 3 * plane + r)
                    wi = rows(par_b.at[j], 5 * plane + r)
                    sr = excl[j, i, 16 * m : 16 * m + 8, :]
                    si = excl[j, i, 16 * m + 8 : 16 * m + 16, :]
                    for k in range(STEPS):
                        keep = m_keep[k]
                        tr, ti = keep * sr, keep * si
                        sr = pr * tr - pi * ti + v[k]
                        si = pr * ti + pi * tr
                        y[k] = y[k] + (wr * sr - wi * si)
                    for n, bit in enumerate((1, 2, 4)):
                        on = (chunk & bit) > 0
                        br = jnp.where(on, rows(derived.at[j], 2 * n * n_rows + r), one)
                        bi = jnp.where(on, rows(derived.at[j], (2 * n + 1) * n_rows + r), zero)
                        wr, wi = cmul(wr, wi, br, bi)
                    table[j, i, 32 * m : 32 * m + 8, :] = wr
                    table[j, i, 32 * m + 8 : 32 * m + 16, :] = wi
                    wr, wi = cmul(wr, wi, pr, pi)
                    table[j, i, 32 * m + 16 : 32 * m + 24, :] = wr
                    table[j, i, 32 * m + 24 : 32 * m + 32, :] = wi
                for k in range(STEPS):
                    gr[j, i, 8 * k : 8 * k + 8, :] = gate[k] * y[k]
                    gm[j, i, 8 * k : 8 * k + 8, :] = gate[k] * m_first[k]

    def finish(j):
        whole_3(j).wait_recv()

        for i2 in range(width // 256):
            halves = []
            for h in range(2):
                i = 2 * i2 + h
                added = None
                for m in range(2):
                    r = 2 * i + m
                    ir = rows(inflow.at[j, i], m)
                    ii = rows(inflow.at[j, i], 2 + m)
                    a1 = rows(derived.at[j], 10 * n_rows + r)
                    a2 = rows(derived.at[j], 11 * n_rows + r)
                    t = [table[j, i, 32 * m + 8 * n : 32 * m + 8 * n + 8, :] for n in range(4)]
                    older = t[0] * ir - t[1] * ii
                    u = [t[2] * ir - t[3] * ii]
                    for k in range(1, STEPS):
                        u.append(a1 * u[-1] - a2 * older)
                        older = u[-2]
                    added = u if added is None else [a + b for a, b in zip(added, u)]
                halves.append(
                    jnp.concatenate(
                        [
                            gr[j, i, 8 * k : 8 * k + 8, :] + gm[j, i, 8 * k : 8 * k + 8, :] * added[k]
                            for k in range(STEPS)
                        ],
                        axis=0,
                    )
                )
            mixed = jnp.concatenate(halves, axis=1).astype(BF16)
            obuf[j, :, i2 * 256 : i2 * 256 + 256] = jnp.dot(perm_out[...], mixed, preferred_element_type=F32).astype(BF16)
        columns = pl.ds(pl.multiple_of(block[j] * width, width), width)
        copy = pltpu.make_async_copy(obuf.at[j], out.at[0, :, columns], o_sem.at[j])
        copy.start()
        return copy

    for j in range(n_dp):
        permute(j)
    products(0)
    if rounds:
        learn(0)
    if len(rounds) > 1:
        tell(1)
    for j in range(1, n_dp):
        send_a(j).wait_recv()
        if j == n_dp - 1:
            for n in range(1, n_dp):
                send_b(n).start()
        products(j)
        if j == 1:

            @pl.when(me > 0)
            def _():
                send_h().wait_recv()

            tiles = half // LANES
            for t in range(tiles):
                both = hrecv[:, t * LANES : (t + 1) * LANES].astype(F32)
                hrows[t] = both[:8]
                hrows[tiles + t] = both[8:]
            states(0)
            gather_plane(0)
        states(j)
        gather_plane(j)
    if len(rounds) > 1:
        learn(1)
    if len(rounds) > 2:
        tell(2)
    response(0)
    for j in range(n_dp):
        combine_plane(j)
    for j in range(1, n_dp):
        send_b(j).wait_recv()
        response(j)
    for j in range(n_dp):
        combine_all(j)
    if far_planes:
        learn(2)
    for j in range(n_dp):
        later_planes(j, far_planes)
    stores = [finish(j) for j in range(n_dp)]

    @pl.when(me + 1 < n_seq)
    def _():
        send_h().wait_send()

    for j in range(n_dp):
        if j:
            send_a(j).wait_send()
            send_b(j).wait_send()
        whole_1(j).wait_send()
        for count in range(1, n_z):

            @pl.when(me_z + count == n_z - 1)
            def _():
                whole_2(j, count).wait_send()

        whole_3(j).wait_send()
    for copy in stores:
        copy.wait()


def local(n_dp, n_seq, streams, short_filter, decay_rate, pole_angle, residue_re, residue_im, skip_gain, doc_starts):
    width = short_filter.shape[2]
    plane = width // LANES
    n_z = n_seq // plane
    n_rows = 2 * plane
    vmem = pltpu.VMEM
    dma = pltpu.SemaphoreType.DMA
    anywhere = pl.BlockSpec(memory_space=pl.ANY)
    return pl.pallas_call(
        functools.partial(kernel, n_dp, n_seq, plane),
        out_shape=jax.ShapeDtypeStruct((1, TOK, streams.shape[3]), BF16),
        in_specs=[anywhere] * 8,
        out_specs=anywhere,
        scratch_shapes=[
            vmem((3, TOK, n_dp * width), BF16),
            vmem((16, n_dp * width // 2), BF16),
            vmem((16, n_dp * width // 2), BF16),
            vmem((16, n_dp * width // 2), F32),
            vmem((n_dp * plane, 8, LANES), F32),
            vmem((n_dp, 2, plane, TOK, LANES), F32),
            vmem((n_dp, plane, 32, LANES), F32),
            vmem((n_dp, TOK, width), BF16),
            vmem((3, 3, width), F32),
            vmem((2, width), F32),
            vmem((2, width), F32),
            vmem((2, width), F32),
            vmem((2, width), F32),
            vmem((1, width), F32),
            vmem((4, n_rows, LANES), F32),
            pltpu.SMEM(doc_starts.shape, jnp.int32),
            vmem((n_dp, 10 * plane, LANES), F32),
            vmem((n_dp, 8 * plane, LANES), F32),
            vmem((n_dp, 16 * n_rows, LANES), F32),
            vmem((TOK, TOK), BF16),
            vmem((TOK, TOK), BF16),
            vmem((STEPS, 8, LANES), F32),
            vmem((STEPS, 8, LANES), F32),
            vmem((2, 8, LANES), F32),
            vmem((STEPS, 8, LANES), F32),
            vmem((3, 8, LANES), F32),
            vmem((2, 8, LANES), F32),
            vmem((n_dp, plane, TOK, LANES), F32),
            vmem((n_dp, plane, TOK, LANES), F32),
            vmem((n_dp, plane, TOK, LANES), F32),
            vmem((n_dp, plane, 32, LANES), F32),
            vmem((n_dp, plane, 64, LANES), F32),
            vmem((n_dp, plane, 4, LANES), F32),
            vmem((n_dp, plane, 4, LANES), F32),
            vmem((n_dp, plane, 4, LANES), F32),
            vmem((n_dp, 4, LANES), F32),
            vmem((n_dp, n_z, 4, LANES), F32),
            vmem((n_dp, plane, 4, LANES), F32),
            vmem((n_dp, plane, 4, LANES), F32),
            dma((7,)),
            dma(()),
            dma((n_dp - 1,)),
            dma((n_dp - 1,)),
            dma((n_dp - 1,)),
            dma((n_dp - 1,)),
            dma(()),
            dma(()),
            dma((n_dp,)),
            dma((n_dp,)),
            dma((n_dp,)),
            dma((n_dp,)),
            dma((n_dp,)),
            dma((n_dp,)),
            dma((n_dp,)),
            pltpu.SemaphoreType.REGULAR((3,)),
        ],
        compiler_params=pltpu.CompilerParams(collective_id=0, has_side_effects=True, vmem_limit_bytes=48 * 2**20),
        name="hyena_modal_scan",
    )(
        *[
            pltpu.with_memory_space_constraint(a, pltpu.HBM)
            for a in (
                streams,
                short_filter,
                decay_rate,
                pole_angle,
                residue_re,
                residue_im,
                skip_gain.reshape(1, width),
                doc_starts,
            )
        ]
    )


def solution(mesh):
    placed = (
        P(None, "dp", "seq", None),
        P(None, None, "dp"),
        P(None, "dp"),
        P(None, "dp"),
        P(None, "dp"),
        P(None, "dp"),
        P("dp"),
        P("dp", None),
    )
    return jax.shard_map(
        functools.partial(local, mesh.shape["dp"], mesh.shape["seq"]),
        mesh=mesh,
        in_specs=placed,
        out_specs=P("dp", "seq", None),
        check_vma=False,
    )
```

```python
import functools

import jax
import jax.numpy as jnp
from jax import lax
from jax.experimental import pallas as pl
from jax.experimental.pallas import tpu as pltpu
from jax.sharding import PartitionSpec as P

MESH = pl.DeviceIdType.MESH
F32 = jnp.float32
BF16 = jnp.bfloat16
LANES = 128
CHUNKS = 8
STEPS = 16
TOK = CHUNKS * STEPS


def iota(shape, axis):
    return lax.broadcasted_iota(jnp.int32, shape, axis)


def rows(ref, row, count=8):
    return jnp.broadcast_to(ref[pl.ds(row, 1), :], (count, LANES))


def cmul(ar, ai, br, bi):
    return ar * br - ai * bi, ar * bi + ai * br


def kernel(
    n_dp,
    n_seq,
    plane,
    streams_hbm,
    taps_hbm,
    decay_hbm,
    angle_hbm,
    resr_hbm,
    resi_hbm,
    skip_hbm,
    starts_hbm,
    out,
    xbuf,
    hsend,
    hrecv,
    hsrc,
    hrows,
    xs,
    ends,
    obuf,
    taps_v,
    decay_v,
    angle_v,
    resr_v,
    resi_v,
    skip_v,
    raw,
    starts_s,
    par_a,
    par_b,
    derived,
    perm_in,
    perm_out,
    m_keep,
    m_tail,
    m_head,
    m_first,
    m_scan,
    m_dev,
    vbuf,
    gr,
    gm,
    excl,
    table,
    state,
    r1,
    pre,
    total,
    r2,
    back,
    inflow,
    in_sem,
    x_sem,
    pa_send,
    pa_recv,
    pb_send,
    pb_recv,
    h_send,
    h_recv,
    s1_send,
    s1_recv,
    s2_send,
    s2_recv,
    s3_send,
    s3_recv,
    o_sem,
    known,
):
    n_z = n_seq // plane
    width = plane * LANES
    me_x = lax.axis_index("dp")
    me = lax.axis_index("seq")
    me_z = me // plane
    me_q = me % plane
    offsets = [0]
    for d in range(1, n_dp // 2 + 1):
        offsets.append(d)
        if n_dp - d != d:
            offsets.append(n_dp - d)

    x_peer = [None] + [((me_x + n_dp - o) % n_dp, me) for o in offsets[1:]]
    q_rank = [(me_q + k) % plane for k in range(1, plane)]
    q_peer = [(me_x, me_z * plane + r) for r in q_rank]
    z_later = [(me_x, (me_z + k) % n_z * plane + me_q) for k in range(1, n_z)]
    after = (me_x, (me + 1) % n_seq)
    before = (me_x, (me + n_seq - 1) % n_seq)
    block = [(me_x + o) % n_dp for o in offsets]

    def z_at(shift):
        return (me_x, (me_z + shift + n_z) % n_z * plane + me_q)

    barrier = pltpu.get_barrier_semaphore()
    for peer in x_peer[1:] + q_peer:
        pl.semaphore_signal(barrier, inc=1, device_id=peer, device_id_type=MESH)
    greeted = jnp.int32(len(x_peer) - 1 + len(q_peer)) + me_z
    for near_by, peer in [(me > 0, before), (me + 1 < n_seq, after)]:
        greeted += jnp.where(near_by, 1, 0)

        @pl.when(near_by)
        def _():
            pl.semaphore_signal(barrier, inc=1, device_id=peer, device_id_type=MESH)

    for k in range(1, n_z):

        @pl.when(me_z + k < n_z)
        def _():
            pl.semaphore_signal(barrier, inc=1, device_id=z_at(k), device_id_type=MESH)

    def tell_earlier():
        for k in range(1, n_z):

            @pl.when(me_z >= k)
            def _():
                pl.semaphore_signal(known, inc=1, device_id=z_at(-k), device_id_type=MESH)

    def learn_later():
        @pl.when(me_z < n_z - 1)
        def _():
            pl.semaphore_wait(known, n_z - 1 - me_z)

    loads = [
        pltpu.make_async_copy(a, b, in_sem.at[n])
        for n, (a, b) in enumerate(
            [
                (taps_hbm, taps_v),
                (decay_hbm, decay_v),
                (angle_hbm, angle_v),
                (resr_hbm, resr_v),
                (resi_hbm, resi_v),
                (skip_hbm, skip_v),
                (starts_hbm, starts_s),
            ]
        )
    ]
    for copy in loads:
        copy.start()
    x_load = pltpu.make_async_copy(streams_hbm.at[:, 0], xbuf, x_sem)
    x_load.start()

    row = iota((TOK, TOK), 0)
    col = iota((TOK, TOK), 1)
    perm_in[...] = jnp.where(col == (row % CHUNKS) * STEPS + row // CHUNKS, 1.0, 0.0).astype(BF16)
    perm_out[...] = jnp.where(col == (row % STEPS) * CHUNKS + row // STEPS, 1.0, 0.0).astype(BF16)

    for copy in loads[:6]:
        copy.wait()
    for i in range(plane):
        lane = slice(i * LANES, (i + 1) * LANES)
        for s in range(2):
            for k in range(3):
                par_a[0, (3 * s + k) * plane + i, :] = taps_v[k, s, lane]
        for k in range(3):
            par_b[0, k * plane + i, :] = taps_v[k, 2, lane]
        par_b[0, 7 * plane + i, :] = skip_v[0, lane]
        for m in range(2):
            r = 2 * i + m
            for n, source in enumerate((decay_v, angle_v, resr_v, resi_v)):
                raw[n, r, :] = source[m, lane]
    decay = raw[0]
    magnitude = jnp.exp(-decay)
    par_a[0, 6 * plane : 8 * plane, :] = magnitude * jnp.cos(raw[1])
    par_a[0, 8 * plane : 10 * plane, :] = magnitude * jnp.sin(raw[1])
    square = decay * decay
    sinh = decay * (1.0 + square * (1.0 / 6.0) * (1.0 + square * (1.0 / 20.0) * (1.0 + square * (1.0 / 42.0))))
    norm = jnp.sqrt(2.0 * magnitude * sinh)
    par_b[0, 3 * plane : 5 * plane, :] = norm * raw[2]
    par_b[0, 5 * plane : 7 * plane, :] = norm * raw[3]

    @pl.when(me == 0)
    def _():
        hrecv[...] = jnp.zeros_like(hrecv)

    hsrc[...] = jnp.zeros_like(hsrc)

    pl.semaphore_wait(barrier, greeted)

    def remote(source, target, send_sem, recv_sem, device):
        return pltpu.make_async_remote_copy(
            src_ref=source, dst_ref=target, send_sem=send_sem, recv_sem=recv_sem, device_id=device, device_id_type=MESH
        )

    def send_a(j):
        return remote(par_a.at[0], par_a.at[j], pa_send.at[j - 1], pa_recv.at[j - 1], x_peer[j])

    def send_b(j):
        return remote(par_b.at[0], par_b.at[j], pb_send.at[j - 1], pb_recv.at[j - 1], x_peer[j])

    for j in range(1, n_dp):
        send_a(j).start()
    tell_earlier()
    x_load.wait()
    half = n_dp * width // 2
    for s in range(3):
        last = xbuf[s, TOK - 16 :, :].astype(F32)[14:16]
        for h in range(2):
            hsrc[8 * h + 2 * s : 8 * h + 2 * s + 2, :] = last[:, h * half : (h + 1) * half]
    hsend[...] = hsrc[...].astype(BF16)

    def send_h():
        return remote(hsend, hrecv, h_send, h_recv, after)

    @pl.when(me + 1 < n_seq)
    def _():
        send_h().start()

    loads[6].wait()
    starts = [starts_s[0, d] for d in range(starts_s.shape[1])]
    near = [s - me * TOK for s in starts]
    chunk = iota((8, LANES), 0)
    one = jnp.ones((8, LANES), F32)
    zero = jnp.zeros((8, LANES), F32)

    def free(lo, hi, among):
        hit = (among[0] >= lo) & (among[0] < hi)
        for s in among[1:]:
            hit = hit | ((s >= lo) & (s < hi))
        return jnp.where(hit, zero, one)

    for k in range(STEPS):
        here = chunk * STEPS + k
        m_keep[k] = free(here, here + 1, near)
        tail = free(here + 1, chunk * STEPS + STEPS, near)
        if k < 2:
            m_head[k] = jnp.where(chunk == 0, tail, zero)
            tail = jnp.where(chunk == 0, zero, tail)
        m_tail[k] = tail
        m_first[k] = free(jnp.zeros_like(here), here + 1, near)
    for n, shift in enumerate((1, 2, 4)):
        reach = free((chunk - shift + 1) * STEPS, (chunk + 1) * STEPS, near)
        m_scan[n] = jnp.where(chunk >= shift, reach, zero)
    first_of_plane = me_z * plane * TOK
    m_dev[0] = free(first_of_plane + chunk * TOK, first_of_plane + (chunk + 1) * TOK, starts)
    m_dev[1] = free(chunk * plane * TOK, (chunk + 1) * plane * TOK, starts)

    n_rows = 2 * plane
    log_plane = plane.bit_length() - 1

    def filters(j, i, source, base, x):
        c = [rows(source.at[j], (base + k) * plane + i) for k in range(3)]
        x = [pltpu.roll(x[STEPS - 2], 1, axis=0), pltpu.roll(x[STEPS - 1], 1, axis=0)] + x
        return [c[0] * x[k + 2] + c[1] * x[k + 1] + c[2] * x[k] for k in range(STEPS)]

    def first_two(j, s, i, source, base, x):
        c = [rows(source.at[j], (base + k) * plane + i) for k in range(3)]
        older = rows(hrows.at[block[j] * plane + i], 2 * s)
        old = rows(hrows.at[block[j] * plane + i], 2 * s + 1)
        return [c[0] * x[0] + c[1] * old + c[2] * older, c[0] * x[1] + c[1] * x[0] + c[2] * old]

    def permuted(j, s, i2):
        lane = pl.ds(pl.multiple_of(block[j] * width + i2 * 256, 256), 256)
        return jnp.dot(perm_in[...], xbuf[s, :, lane], preferred_element_type=F32)

    def permute(j):
        for i2 in range(width // 256):
            for s in range(3):
                x = permuted(j, s, i2)
                xs[j, s, 2 * i2] = x[:, :LANES]
                xs[j, s, 2 * i2 + 1] = x[:, LANES:]

    def steps_of(ref, count=STEPS):
        return [ref[8 * k : 8 * k + 8, :] for k in range(count)]

    def powers(j):
        pr = par_a[j, 6 * plane : 8 * plane, :]
        pi = par_a[j, 8 * plane : 10 * plane, :]
        qr, qi = pr, pi
        tr, ti = pr, pi
        slot = 0
        for n in range(7 + log_plane):
            qr, qi = qr * qr - qi * qi, 2.0 * qr * qi
            if n == 0:
                tr, ti = qr, qi
            elif n < 3:
                tr, ti = cmul(tr, ti, qr, qi)
            if n + 1 in (4, 5, 6, 7, 7 + log_plane):
                derived[j, slot * n_rows : (slot + 1) * n_rows, :] = qr
                derived[j, (slot + 1) * n_rows : (slot + 2) * n_rows, :] = qi
                slot += 2
        derived[j, 10 * n_rows : 11 * n_rows, :] = 2.0 * pr
        derived[j, 11 * n_rows : 12 * n_rows, :] = pr * pr + pi * pi
        derived[j, 12 * n_rows : 13 * n_rows, :] = tr
        derived[j, 13 * n_rows : 14 * n_rows, :] = ti
        tr, ti = cmul(tr, ti, pr, pi)
        derived[j, 14 * n_rows : 15 * n_rows, :] = tr
        derived[j, 15 * n_rows : 16 * n_rows, :] = ti

    def products(j):
        powers(j)

        @pl.loop(0, plane // 2)
        def _(i2):
            for i in (2 * i2, 2 * i2 + 1):
                f0 = filters(j, i, par_a, 0, steps_of(xs.at[j, 0, i]))
                f1 = filters(j, i, par_a, 3, steps_of(xs.at[j, 1, i]))
                masked = []
                for k in range(STEPS):
                    v = f0[k] * f1[k]
                    vbuf[j, i, 8 * k : 8 * k + 8, :] = v
                    masked.append(v * m_tail[k])
                for m in range(2):
                    r = 2 * i + m
                    a1 = rows(derived.at[j], 10 * n_rows + r)
                    a2 = rows(derived.at[j], 11 * n_rows + r)
                    b2, b1 = masked[0], a1 * masked[0] + masked[1]
                    for k in range(2, STEPS):
                        b1, b2 = a1 * b1 + (masked[k] - a2 * b2), b1
                    ends[j, i, 16 * m : 16 * m + 8, :] = b1 - rows(par_a.at[j], 6 * plane + r) * b2
                    ends[j, i, 16 * m + 8 : 16 * m + 16, :] = rows(par_a.at[j], 8 * plane + r) * b2

    def states(j):
        @pl.loop(0, plane // 2)
        def _(i2):
            for i in (2 * i2, 2 * i2 + 1):
                f0 = first_two(j, 0, i, par_a, 0, steps_of(xs.at[j, 0, i], 2))
                f1 = first_two(j, 1, i, par_a, 3, steps_of(xs.at[j, 1, i], 2))
                v = [f0[k] * f1[k] for k in range(2)]
                for k in range(2):
                    vbuf[j, i, 8 * k : 8 * k + 8, :] = jnp.where(
                        chunk == 0, v[k], vbuf[j, i, 8 * k : 8 * k + 8, :]
                    )
                v = [v[k] * m_head[k] for k in range(2)]
                for m in range(2):
                    r = 2 * i + m
                    p14, q14, p15, q15 = [rows(derived.at[j], (12 + n) * n_rows + r) for n in range(4)]
                    er = ends[j, i, 16 * m : 16 * m + 8, :] + (v[0] * p15 + v[1] * p14)
                    ei = ends[j, i, 16 * m + 8 : 16 * m + 16, :] + (v[0] * q15 + v[1] * q14)
                    for n, shift in enumerate((1, 2, 4)):
                        reach = m_scan[n]
                        kr = reach * rows(derived.at[j], 2 * n * n_rows + r)
                        ki = reach * rows(derived.at[j], (2 * n + 1) * n_rows + r)
                        sr = pltpu.roll(er, shift, axis=0)
                        si = pltpu.roll(ei, shift, axis=0)
                        ar, ai = cmul(kr, ki, sr, si)
                        er, ei = er + ar, ei + ai
                    state[j, i, pl.ds(m, 1), :] = er[7:8]
                    state[j, i, pl.ds(2 + m, 1), :] = ei[7:8]
                    later = jnp.where(chunk >= 1, one, zero)
                    excl[j, i, 16 * m : 16 * m + 8, :] = pltpu.roll(er, 1, axis=0) * later
                    excl[j, i, 16 * m + 8 : 16 * m + 16, :] = pltpu.roll(ei, 1, axis=0) * later

    def gather_plane(j):
        r1[j, me_q] = state[j, me_q]
        for n in range(plane - 1):
            remote(state.at[j, q_rank[n]], r1.at[j, me_q], s1_send, s1_recv.at[j], q_peer[n]).start()

    def whole_1(j):
        others = pl.ds(0, plane - 1)
        return remote(state.at[j, others], r1.at[j, others], s1_send, s1_recv.at[j], q_peer[0])

    def whole_3(j):
        others = pl.ds(0, plane - 1)
        return remote(back.at[j, others], inflow.at[j, others], s3_send, s3_recv.at[j], q_peer[0])

    def send_2(j, k):
        return remote(total.at[j], r2.at[j, me_z], s2_send, s2_recv.at[j], z_later[k - 1])

    def later_planes(j):
        for k in range(1, n_z):

            @pl.when(me_z + k < n_z)
            def _():
                send_2(j, k).start()

    def whole_2(j, count):
        those = pl.ds(0, count)
        return remote(r2.at[j, those], r2.at[j, those], s2_send, s2_recv.at[j], z_later[0])

    def combine_plane(j):
        whole_1(j).wait_recv()
        pr = derived[j, pl.ds(6 * n_rows + 2 * me_q, 2), :]
        pi = derived[j, pl.ds(7 * n_rows + 2 * me_q, 2), :]
        run_r = jnp.zeros((2, LANES), F32)
        run_i = run_r
        for e in range(plane):
            pre[j, e, 0:2, :] = run_r
            pre[j, e, 2:4, :] = run_i
            keep = m_dev[0, e : e + 1, :]
            ar, ai = cmul(pr * keep, pi * keep, run_r, run_i)
            run_r = ar + r1[j, e, 0:2, :]
            run_i = ai + r1[j, e, 2:4, :]
        total[j, 0:2, :] = run_r
        total[j, 2:4, :] = run_i
        later_planes(j)

    def combine_all(j):
        for count in range(1, n_z):

            @pl.when(me_z == count)
            def _():
                whole_2(j, count).wait_recv()

        pr = derived[j, pl.ds(8 * n_rows + 2 * me_q, 2), :]
        pi = derived[j, pl.ds(9 * n_rows + 2 * me_q, 2), :]
        run_r = jnp.zeros((2, LANES), F32)
        run_i = run_r
        for z in range(n_z - 1):
            keep = m_dev[1, z : z + 1, :]
            ar, ai = cmul(pr * keep, pi * keep, run_r, run_i)
            past = z < me_z
            run_r = jnp.where(past, ar + r2[j, z, 0:2, :], run_r)
            run_i = jnp.where(past, ai + r2[j, z, 2:4, :], run_i)
        pr = derived[j, pl.ds(6 * n_rows + 2 * me_q, 2), :]
        pi = derived[j, pl.ds(7 * n_rows + 2 * me_q, 2), :]
        for e in range(plane):
            back[j, e, 0:2, :] = pre[j, e, 0:2, :] + run_r
            back[j, e, 2:4, :] = pre[j, e, 2:4, :] + run_i
            keep = m_dev[0, e : e + 1, :]
            run_r, run_i = cmul(pr * keep, pi * keep, run_r, run_i)
        inflow[j, me_q] = back[j, me_q]
        for n in range(plane - 1):
            remote(back.at[j, q_rank[n]], inflow.at[j, me_q], s3_send, s3_recv.at[j], q_peer[n]).start()

    def response(j):
        @pl.loop(0, width // 256)
        def _(i2):
            for h in range(2):
                i = 2 * i2 + h
                x = steps_of(xs.at[j, 2, i])
                gate = filters(j, i, par_b, 0, x)
                head = first_two(j, 2, i, par_b, 0, x)
                for k in range(2):
                    gate[k] = jnp.where(chunk == 0, head[k], gate[k])
                skip = rows(par_b.at[j], 7 * plane + i)
                v = [vbuf[j, i, 8 * k : 8 * k + 8, :] for k in range(STEPS)]
                y = [skip * v[k] for k in range(STEPS)]
                for m in range(2):
                    r = 2 * i + m
                    pr = rows(par_a.at[j], 6 * plane + r)
                    pi = rows(par_a.at[j], 8 * plane + r)
                    wr = rows(par_b.at[j], 3 * plane + r)
                    wi = rows(par_b.at[j], 5 * plane + r)
                    sr = excl[j, i, 16 * m : 16 * m + 8, :]
                    si = excl[j, i, 16 * m + 8 : 16 * m + 16, :]
                    for k in range(STEPS):
                        keep = m_keep[k]
                        tr, ti = keep * sr, keep * si
                        sr = pr * tr - pi * ti + v[k]
                        si = pr * ti + pi * tr
                        y[k] = y[k] + (wr * sr - wi * si)
                    for n, bit in enumerate((1, 2, 4)):
                        on = (chunk & bit) > 0
                        br = jnp.where(on, rows(derived.at[j], 2 * n * n_rows + r), one)
                        bi = jnp.where(on, rows(derived.at[j], (2 * n + 1) * n_rows + r), zero)
                        wr, wi = cmul(wr, wi, br, bi)
                    table[j, i, 32 * m : 32 * m + 8, :] = wr
                    table[j, i, 32 * m + 8 : 32 * m + 16, :] = wi
                    wr, wi = cmul(wr, wi, pr, pi)
                    table[j, i, 32 * m + 16 : 32 * m + 24, :] = wr
                    table[j, i, 32 * m + 24 : 32 * m + 32, :] = wi
                for k in range(STEPS):
                    gr[j, i, 8 * k : 8 * k + 8, :] = gate[k] * y[k]
                    gm[j, i, 8 * k : 8 * k + 8, :] = gate[k] * m_first[k]

    def finish(j):
        whole_3(j).wait_recv()

        for i2 in range(width // 256):
            halves = []
            for h in range(2):
                i = 2 * i2 + h
                added = None
                for m in range(2):
                    r = 2 * i + m
                    ir = rows(inflow.at[j, i], m)
                    ii = rows(inflow.at[j, i], 2 + m)
                    a1 = rows(derived.at[j], 10 * n_rows + r)
                    a2 = rows(derived.at[j], 11 * n_rows + r)
                    t = [table[j, i, 32 * m + 8 * n : 32 * m + 8 * n + 8, :] for n in range(4)]
                    older = t[0] * ir - t[1] * ii
                    u = [t[2] * ir - t[3] * ii]
                    for k in range(1, STEPS):
                        u.append(a1 * u[-1] - a2 * older)
                        older = u[-2]
                    added = u if added is None else [a + b for a, b in zip(added, u)]
                halves.append(
                    jnp.concatenate(
                        [
                            gr[j, i, 8 * k : 8 * k + 8, :] + gm[j, i, 8 * k : 8 * k + 8, :] * added[k]
                            for k in range(STEPS)
                        ],
                        axis=0,
                    )
                )
            mixed = jnp.concatenate(halves, axis=1).astype(BF16)
            lane = pl.ds(pl.multiple_of(block[j] * width + i2 * 256, 256), 256)
            obuf[:, lane] = jnp.dot(perm_out[...], mixed, preferred_element_type=F32).astype(BF16)
        columns = pl.ds(pl.multiple_of(block[j] * width, width), width)
        pltpu.make_async_copy(obuf.at[:, columns], out.at[0, :, columns], o_sem).start()

    for j in range(n_dp):
        permute(j)
    products(0)
    for j in range(1, n_dp):
        send_a(j).wait_recv()
        if j == n_dp - 1:
            for n in range(1, n_dp):
                send_b(n).start()
        products(j)
        if j == 1:

            @pl.when(me > 0)
            def _():
                send_h().wait_recv()

            tiles = half // LANES
            for t in range(tiles):
                both = hrecv[:, t * LANES : (t + 1) * LANES].astype(F32)
                hrows[t] = both[:8]
                hrows[tiles + t] = both[8:]
            states(0)
            gather_plane(0)
        states(j)
        gather_plane(j)
    response(0)
    learn_later()
    for j in range(n_dp):
        combine_plane(j)
    for j in range(1, n_dp):
        send_b(j).wait_recv()
        if j == n_dp - 1:
            combine_all(0)
        response(j)
    for j in range(1, n_dp):
        combine_all(j)
    for j in range(n_dp):
        finish(j)

    @pl.when(me + 1 < n_seq)
    def _():
        send_h().wait_send()

    for j in range(1, n_dp):
        send_a(j).wait_send()
    for j in range(1, n_dp):
        send_b(j).wait_send()
    others = pl.ds(0, plane - 1)
    for source, target, sem in ((state, r1, s1_send), (back, inflow, s3_send)):
        remote(source.at[:, others], target.at[:, others], sem, s1_recv.at[0], q_peer[0]).wait_send()
    for count in range(1, n_z):

        @pl.when(n_z - 1 - me_z == count)
        def _():
            those = r2.at[:, pl.ds(0, count)]
            remote(those, those, s2_send, s2_recv.at[0], z_later[0]).wait_send()

    pltpu.make_async_copy(obuf, out.at[0], o_sem).wait()


def local(n_dp, n_seq, streams, short_filter, decay_rate, pole_angle, residue_re, residue_im, skip_gain, doc_starts):
    width = short_filter.shape[2]
    plane = width // LANES
    n_z = n_seq // plane
    n_rows = 2 * plane
    vmem = pltpu.VMEM
    dma = pltpu.SemaphoreType.DMA
    anywhere = pl.BlockSpec(memory_space=pl.ANY)
    return pl.pallas_call(
        functools.partial(kernel, n_dp, n_seq, plane),
        out_shape=jax.ShapeDtypeStruct((1, TOK, streams.shape[3]), BF16),
        in_specs=[anywhere] * 8,
        out_specs=anywhere,
        scratch_shapes=[
            vmem((3, TOK, n_dp * width), BF16),
            vmem((16, n_dp * width // 2), BF16),
            vmem((16, n_dp * width // 2), BF16),
            vmem((16, n_dp * width // 2), F32),
            vmem((n_dp * plane, 8, LANES), F32),
            vmem((n_dp, 3, plane, TOK, LANES), F32),
            vmem((n_dp, plane, 32, LANES), F32),
            vmem((TOK, n_dp * width), BF16),
            vmem((3, 3, width), F32),
            vmem((2, width), F32),
            vmem((2, width), F32),
            vmem((2, width), F32),
            vmem((2, width), F32),
            vmem((1, width), F32),
            vmem((4, n_rows, LANES), F32),
            pltpu.SMEM(doc_starts.shape, jnp.int32),
            vmem((n_dp, 10 * plane, LANES), F32),
            vmem((n_dp, 8 * plane, LANES), F32),
            vmem((n_dp, 16 * n_rows, LANES), F32),
            vmem((TOK, TOK), BF16),
            vmem((TOK, TOK), BF16),
            vmem((STEPS, 8, LANES), F32),
            vmem((STEPS, 8, LANES), F32),
            vmem((2, 8, LANES), F32),
            vmem((STEPS, 8, LANES), F32),
            vmem((3, 8, LANES), F32),
            vmem((2, 8, LANES), F32),
            vmem((n_dp, plane, TOK, LANES), F32),
            vmem((n_dp, plane, TOK, LANES), F32),
            vmem((n_dp, plane, TOK, LANES), F32),
            vmem((n_dp, plane, 32, LANES), F32),
            vmem((n_dp, plane, 64, LANES), F32),
            vmem((n_dp, plane, 4, LANES), F32),
            vmem((n_dp, plane, 4, LANES), F32),
            vmem((n_dp, plane, 4, LANES), F32),
            vmem((n_dp, 4, LANES), F32),
            vmem((n_dp, n_z, 4, LANES), F32),
            vmem((n_dp, plane, 4, LANES), F32),
            vmem((n_dp, plane, 4, LANES), F32),
            dma((7,)),
            dma(()),
            dma((n_dp - 1,)),
            dma((n_dp - 1,)),
            dma((n_dp - 1,)),
            dma((n_dp - 1,)),
            dma(()),
            dma(()),
            dma(()),
            dma((n_dp,)),
            dma(()),
            dma((n_dp,)),
            dma(()),
            dma((n_dp,)),
            dma(()),
            pltpu.SemaphoreType.REGULAR,
        ],
        compiler_params=pltpu.CompilerParams(collective_id=0, has_side_effects=True, vmem_limit_bytes=48 * 2**20),
        name="hyena_modal_scan",
    )(
        *[
            pltpu.with_memory_space_constraint(a, pltpu.HBM)
            for a in (
                streams,
                short_filter,
                decay_rate,
                pole_angle,
                residue_re,
                residue_im,
                skip_gain.reshape(1, width),
                doc_starts,
            )
        ]
    )


def solution(mesh):
    placed = (
        P(None, "dp", "seq", None),
        P(None, None, "dp"),
        P(None, "dp"),
        P(None, "dp"),
        P(None, "dp"),
        P(None, "dp"),
        P("dp"),
        P("dp", None),
    )
    return jax.shard_map(
        functools.partial(local, mesh.shape["dp"], mesh.shape["seq"]),
        mesh=mesh,
        in_specs=placed,
        out_specs=P("dp", "seq", None),
        check_vma=False,
    )
```

```python
import functools

import jax
import jax.numpy as jnp
from jax import lax
from jax.experimental import pallas as pl
from jax.experimental.pallas import tpu as pltpu
from jax.sharding import PartitionSpec as P

MESH = pl.DeviceIdType.MESH
F32 = jnp.float32
BF16 = jnp.bfloat16
LANES = 128
CHUNKS = 8
STEPS = 16
TOK = CHUNKS * STEPS


def iota(shape, axis):
    return lax.broadcasted_iota(jnp.int32, shape, axis)


def rows(ref, row, count=8):
    return jnp.broadcast_to(ref[pl.ds(row, 1), :], (count, LANES))


def cmul(ar, ai, br, bi):
    return ar * br - ai * bi, ar * bi + ai * br


def kernel(
    n_dp,
    n_seq,
    plane,
    streams_hbm,
    taps_hbm,
    decay_hbm,
    angle_hbm,
    resr_hbm,
    resi_hbm,
    skip_hbm,
    starts_hbm,
    out,
    xbuf,
    hsend,
    hrecv,
    hsrc,
    hrows,
    xs,
    ends,
    obuf,
    taps_v,
    decay_v,
    angle_v,
    resr_v,
    resi_v,
    skip_v,
    raw,
    starts_s,
    par_a,
    par_b,
    derived,
    perm_in,
    perm_out,
    m_keep,
    m_tail,
    m_head,
    m_first,
    m_scan,
    m_dev,
    vbuf,
    gr,
    gm,
    excl,
    table,
    state,
    r1,
    pre,
    total,
    r2,
    back,
    inflow,
    in_sem,
    x_sem,
    pa_send,
    pa_recv,
    pb_send,
    pb_recv,
    h_send,
    h_recv,
    s1_send,
    s1_recv,
    s2_send,
    s2_recv,
    s3_send,
    s3_recv,
    o_sem,
    known,
):
    n_z = n_seq // plane
    width = plane * LANES
    me_x = lax.axis_index("dp")
    me = lax.axis_index("seq")
    me_z = me // plane
    me_q = me % plane
    offsets = [0]
    for d in range(1, n_dp // 2 + 1):
        offsets.append(d)
        if n_dp - d != d:
            offsets.append(n_dp - d)

    x_peer = [None] + [((me_x + n_dp - o) % n_dp, me) for o in offsets[1:]]
    q_rank = [(me_q + k) % plane for k in range(1, plane)]
    q_peer = [(me_x, me_z * plane + r) for r in q_rank]
    z_later = [(me_x, (me_z + k) % n_z * plane + me_q) for k in range(1, n_z)]
    after = (me_x, (me + 1) % n_seq)
    before = (me_x, (me + n_seq - 1) % n_seq)
    block = [(me_x + o) % n_dp for o in offsets]

    def z_at(shift):
        return (me_x, (me_z + shift + n_z) % n_z * plane + me_q)

    barrier = pltpu.get_barrier_semaphore()
    for peer in x_peer[1:] + q_peer:
        pl.semaphore_signal(barrier, inc=1, device_id=peer, device_id_type=MESH)
    greeted = jnp.int32(len(x_peer) - 1 + len(q_peer)) + me_z
    for near_by, peer in [(me > 0, before), (me + 1 < n_seq, after)]:
        greeted += jnp.where(near_by, 1, 0)

        @pl.when(near_by)
        def _():
            pl.semaphore_signal(barrier, inc=1, device_id=peer, device_id_type=MESH)

    for k in range(1, n_z):

        @pl.when(me_z + k < n_z)
        def _():
            pl.semaphore_signal(barrier, inc=1, device_id=z_at(k), device_id_type=MESH)

    def tell_earlier():
        for k in range(1, n_z):

            @pl.when(me_z >= k)
            def _():
                pl.semaphore_signal(known, inc=1, device_id=z_at(-k), device_id_type=MESH)

    def learn_later():
        @pl.when(me_z < n_z - 1)
        def _():
            pl.semaphore_wait(known, n_z - 1 - me_z)

    loads = [
        pltpu.make_async_copy(a, b, in_sem.at[n])
        for n, (a, b) in enumerate(
            [
                (taps_hbm, taps_v),
                (decay_hbm, decay_v),
                (angle_hbm, angle_v),
                (resr_hbm, resr_v),
                (resi_hbm, resi_v),
                (skip_hbm, skip_v),
                (starts_hbm, starts_s),
            ]
        )
    ]
    for copy in loads:
        copy.start()
    x_load = pltpu.make_async_copy(streams_hbm.at[:, 0], xbuf, x_sem)
    x_load.start()

    row = iota((TOK, TOK), 0)
    col = iota((TOK, TOK), 1)
    perm_in[...] = jnp.where(col == (row % CHUNKS) * STEPS + row // CHUNKS, 1.0, 0.0).astype(BF16)
    perm_out[...] = jnp.where(col == (row % STEPS) * CHUNKS + row // STEPS, 1.0, 0.0).astype(BF16)

    for copy in loads[:6]:
        copy.wait()
    for i in range(plane):
        lane = slice(i * LANES, (i + 1) * LANES)
        for s in range(2):
            for k in range(3):
                par_a[0, (3 * s + k) * plane + i, :] = taps_v[k, s, lane]
        for k in range(3):
            par_b[0, k * plane + i, :] = taps_v[k, 2, lane]
        par_b[0, 7 * plane + i, :] = skip_v[0, lane]
        for m in range(2):
            r = 2 * i + m
            for n, source in enumerate((decay_v, angle_v, resr_v, resi_v)):
                raw[n, r, :] = source[m, lane]
    decay = raw[0]
    magnitude = jnp.exp(-decay)
    par_a[0, 6 * plane : 8 * plane, :] = magnitude * jnp.cos(raw[1])
    par_a[0, 8 * plane : 10 * plane, :] = magnitude * jnp.sin(raw[1])
    square = decay * decay
    sinh = decay * (1.0 + square * (1.0 / 6.0) * (1.0 + square * (1.0 / 20.0) * (1.0 + square * (1.0 / 42.0))))
    norm = jnp.sqrt(2.0 * magnitude * sinh)
    par_b[0, 3 * plane : 5 * plane, :] = norm * raw[2]
    par_b[0, 5 * plane : 7 * plane, :] = norm * raw[3]

    @pl.when(me == 0)
    def _():
        hrecv[...] = jnp.zeros_like(hrecv)

    hsrc[...] = jnp.zeros_like(hsrc)

    pl.semaphore_wait(barrier, greeted)

    def remote(source, target, send_sem, recv_sem, device):
        return pltpu.make_async_remote_copy(
            src_ref=source, dst_ref=target, send_sem=send_sem, recv_sem=recv_sem, device_id=device, device_id_type=MESH
        )

    def send_a(j):
        return remote(par_a.at[0], par_a.at[j], pa_send.at[j - 1], pa_recv.at[j - 1], x_peer[j])

    def send_b(j):
        return remote(par_b.at[0], par_b.at[j], pb_send.at[j - 1], pb_recv.at[j - 1], x_peer[j])

    for j in range(1, n_dp):
        send_a(j).start()
    tell_earlier()
    x_load.wait()
    half = n_dp * width // 2
    for s in range(3):
        last = xbuf[s, TOK - 16 :, :].astype(F32)[14:16]
        for h in range(2):
            hsrc[8 * h + 2 * s : 8 * h + 2 * s + 2, :] = last[:, h * half : (h + 1) * half]
    hsend[...] = hsrc[...].astype(BF16)

    def send_h():
        return remote(hsend, hrecv, h_send, h_recv, after)

    @pl.when(me + 1 < n_seq)
    def _():
        send_h().start()

    loads[6].wait()
    starts = [starts_s[0, d] for d in range(starts_s.shape[1])]
    near = [s - me * TOK for s in starts]
    chunk = iota((8, LANES), 0)
    one = jnp.ones((8, LANES), F32)
    zero = jnp.zeros((8, LANES), F32)

    def free(lo, hi, among):
        hit = (among[0] >= lo) & (among[0] < hi)
        for s in among[1:]:
            hit = hit | ((s >= lo) & (s < hi))
        return jnp.where(hit, zero, one)

    for k in range(STEPS):
        here = chunk * STEPS + k
        m_keep[k] = free(here, here + 1, near)
        tail = free(here + 1, chunk * STEPS + STEPS, near)
        if k < 2:
            m_head[k] = jnp.where(chunk == 0, tail, zero)
            tail = jnp.where(chunk == 0, zero, tail)
        m_tail[k] = tail
        m_first[k] = free(jnp.zeros_like(here), here + 1, near)
    for n, shift in enumerate((1, 2, 4)):
        reach = free((chunk - shift + 1) * STEPS, (chunk + 1) * STEPS, near)
        m_scan[n] = jnp.where(chunk >= shift, reach, zero)
    first_of_plane = me_z * plane * TOK
    m_dev[0] = free(first_of_plane + chunk * TOK, first_of_plane + (chunk + 1) * TOK, starts)
    m_dev[1] = free(chunk * plane * TOK, (chunk + 1) * plane * TOK, starts)

    n_rows = 2 * plane
    log_plane = plane.bit_length() - 1

    def filters(j, i, source, base, x):
        c = [rows(source.at[j], (base + k) * plane + i) for k in range(3)]
        x = [pltpu.roll(x[STEPS - 2], 1, axis=0), pltpu.roll(x[STEPS - 1], 1, axis=0)] + x
        return [c[0] * x[k + 2] + c[1] * x[k + 1] + c[2] * x[k] for k in range(STEPS)]

    def first_two(j, s, i, source, base, x):
        c = [rows(source.at[j], (base + k) * plane + i) for k in range(3)]
        older = rows(hrows.at[block[j] * plane + i], 2 * s)
        old = rows(hrows.at[block[j] * plane + i], 2 * s + 1)
        return [c[0] * x[0] + c[1] * old + c[2] * older, c[0] * x[1] + c[1] * x[0] + c[2] * old]

    def permuted(j, s, i2):
        lane = pl.ds(pl.multiple_of(block[j] * width + i2 * 256, 256), 256)
        return jnp.dot(perm_in[...], xbuf[s, :, lane], preferred_element_type=F32)

    def permute(j):
        for i2 in range(width // 256):
            for s in range(3):
                x = permuted(j, s, i2)
                xs[j, s, 2 * i2] = x[:, :LANES]
                xs[j, s, 2 * i2 + 1] = x[:, LANES:]

    def steps_of(ref, count=STEPS):
        return [ref[8 * k : 8 * k + 8, :] for k in range(count)]

    def powers(j):
        pr = par_a[j, 6 * plane : 8 * plane, :]
        pi = par_a[j, 8 * plane : 10 * plane, :]
        qr, qi = pr, pi
        tr, ti = pr, pi
        slot = 0
        for n in range(7 + log_plane):
            qr, qi = qr * qr - qi * qi, 2.0 * qr * qi
            if n == 0:
                tr, ti = qr, qi
            elif n < 3:
                tr, ti = cmul(tr, ti, qr, qi)
            if n + 1 in (4, 5, 6, 7, 7 + log_plane):
                derived[j, slot * n_rows : (slot + 1) * n_rows, :] = qr
                derived[j, (slot + 1) * n_rows : (slot + 2) * n_rows, :] = qi
                slot += 2
        derived[j, 10 * n_rows : 11 * n_rows, :] = 2.0 * pr
        derived[j, 11 * n_rows : 12 * n_rows, :] = pr * pr + pi * pi
        derived[j, 12 * n_rows : 13 * n_rows, :] = tr
        derived[j, 13 * n_rows : 14 * n_rows, :] = ti
        tr, ti = cmul(tr, ti, pr, pi)
        derived[j, 14 * n_rows : 15 * n_rows, :] = tr
        derived[j, 15 * n_rows : 16 * n_rows, :] = ti

    def products(j):
        powers(j)

        @pl.loop(0, plane // 2)
        def _(i2):
            for i in (2 * i2, 2 * i2 + 1):
                f0 = filters(j, i, par_a, 0, steps_of(xs.at[j, 0, i]))
                f1 = filters(j, i, par_a, 3, steps_of(xs.at[j, 1, i]))
                masked = []
                for k in range(STEPS):
                    v = f0[k] * f1[k]
                    vbuf[j, i, 8 * k : 8 * k + 8, :] = v
                    masked.append(v * m_tail[k])
                for m in range(2):
                    r = 2 * i + m
                    a1 = rows(derived.at[j], 10 * n_rows + r)
                    a2 = rows(derived.at[j], 11 * n_rows + r)
                    b2, b1 = masked[0], a1 * masked[0] + masked[1]
                    for k in range(2, STEPS):
                        b1, b2 = a1 * b1 + (masked[k] - a2 * b2), b1
                    ends[j, i, 16 * m : 16 * m + 8, :] = b1 - rows(par_a.at[j], 6 * plane + r) * b2
                    ends[j, i, 16 * m + 8 : 16 * m + 16, :] = rows(par_a.at[j], 8 * plane + r) * b2

    def states(j):
        @pl.loop(0, plane // 2)
        def _(i2):
            for i in (2 * i2, 2 * i2 + 1):
                f0 = first_two(j, 0, i, par_a, 0, steps_of(xs.at[j, 0, i], 2))
                f1 = first_two(j, 1, i, par_a, 3, steps_of(xs.at[j, 1, i], 2))
                v = [f0[k] * f1[k] for k in range(2)]
                for k in range(2):
                    vbuf[j, i, 8 * k : 8 * k + 8, :] = jnp.where(
                        chunk == 0, v[k], vbuf[j, i, 8 * k : 8 * k + 8, :]
                    )
                v = [v[k] * m_head[k] for k in range(2)]
                for m in range(2):
                    r = 2 * i + m
                    p14, q14, p15, q15 = [rows(derived.at[j], (12 + n) * n_rows + r) for n in range(4)]
                    er = ends[j, i, 16 * m : 16 * m + 8, :] + (v[0] * p15 + v[1] * p14)
                    ei = ends[j, i, 16 * m + 8 : 16 * m + 16, :] + (v[0] * q15 + v[1] * q14)
                    for n, shift in enumerate((1, 2, 4)):
                        reach = m_scan[n]
                        kr = reach * rows(derived.at[j], 2 * n * n_rows + r)
                        ki = reach * rows(derived.at[j], (2 * n + 1) * n_rows + r)
                        sr = pltpu.roll(er, shift, axis=0)
                        si = pltpu.roll(ei, shift, axis=0)
                        ar, ai = cmul(kr, ki, sr, si)
                        er, ei = er + ar, ei + ai
                    state[j, i, pl.ds(m, 1), :] = er[7:8]
                    state[j, i, pl.ds(2 + m, 1), :] = ei[7:8]
                    later = jnp.where(chunk >= 1, one, zero)
                    excl[j, i, 16 * m : 16 * m + 8, :] = pltpu.roll(er, 1, axis=0) * later
                    excl[j, i, 16 * m + 8 : 16 * m + 16, :] = pltpu.roll(ei, 1, axis=0) * later

    def gather_plane(j):
        r1[j, me_q] = state[j, me_q]
        for n in range(plane - 1):
            remote(state.at[j, q_rank[n]], r1.at[j, me_q], s1_send, s1_recv.at[j], q_peer[n]).start()

    def whole_1(j):
        others = pl.ds(0, plane - 1)
        return remote(state.at[j, others], r1.at[j, others], s1_send, s1_recv.at[j], q_peer[0])

    def whole_3(j):
        others = pl.ds(0, plane - 1)
        return remote(back.at[j, others], inflow.at[j, others], s3_send, s3_recv.at[j], q_peer[0])

    def send_2(j, k):
        return remote(total.at[j], r2.at[j, me_z], s2_send, s2_recv.at[j], z_later[k - 1])

    def later_planes(j):
        for k in range(1, n_z):

            @pl.when(me_z + k < n_z)
            def _():
                send_2(j, k).start()

    def whole_2(j, count):
        those = pl.ds(0, count)
        return remote(r2.at[j, those], r2.at[j, those], s2_send, s2_recv.at[j], z_later[0])

    def combine_plane(j):
        whole_1(j).wait_recv()
        pr = derived[j, pl.ds(6 * n_rows + 2 * me_q, 2), :]
        pi = derived[j, pl.ds(7 * n_rows + 2 * me_q, 2), :]
        run_r = jnp.zeros((2, LANES), F32)
        run_i = run_r
        for e in range(plane):
            pre[j, e, 0:2, :] = run_r
            pre[j, e, 2:4, :] = run_i
            keep = m_dev[0, e : e + 1, :]
            ar, ai = cmul(pr * keep, pi * keep, run_r, run_i)
            run_r = ar + r1[j, e, 0:2, :]
            run_i = ai + r1[j, e, 2:4, :]
        total[j, 0:2, :] = run_r
        total[j, 2:4, :] = run_i
        later_planes(j)

    def combine_all(j):
        for count in range(1, n_z):

            @pl.when(me_z == count)
            def _():
                whole_2(j, count).wait_recv()

        pr = derived[j, pl.ds(8 * n_rows + 2 * me_q, 2), :]
        pi = derived[j, pl.ds(9 * n_rows + 2 * me_q, 2), :]
        run_r = jnp.zeros((2, LANES), F32)
        run_i = run_r
        for z in range(n_z - 1):
            keep = m_dev[1, z : z + 1, :]
            ar, ai = cmul(pr * keep, pi * keep, run_r, run_i)
            past = z < me_z
            run_r = jnp.where(past, ar + r2[j, z, 0:2, :], run_r)
            run_i = jnp.where(past, ai + r2[j, z, 2:4, :], run_i)
        pr = derived[j, pl.ds(6 * n_rows + 2 * me_q, 2), :]
        pi = derived[j, pl.ds(7 * n_rows + 2 * me_q, 2), :]
        for e in range(plane):
            back[j, e, 0:2, :] = pre[j, e, 0:2, :] + run_r
            back[j, e, 2:4, :] = pre[j, e, 2:4, :] + run_i
            keep = m_dev[0, e : e + 1, :]
            run_r, run_i = cmul(pr * keep, pi * keep, run_r, run_i)
        inflow[j, me_q] = back[j, me_q]
        for n in range(plane - 1):
            remote(back.at[j, q_rank[n]], inflow.at[j, me_q], s3_send, s3_recv.at[j], q_peer[n]).start()

    def response(j):
        @pl.loop(0, width // 256)
        def _(i2):
            for h in range(2):
                i = 2 * i2 + h
                x = steps_of(xs.at[j, 2, i])
                gate = filters(j, i, par_b, 0, x)
                head = first_two(j, 2, i, par_b, 0, x)
                for k in range(2):
                    gate[k] = jnp.where(chunk == 0, head[k], gate[k])
                skip = rows(par_b.at[j], 7 * plane + i)
                v = [vbuf[j, i, 8 * k : 8 * k + 8, :] for k in range(STEPS)]
                y = [skip * v[k] for k in range(STEPS)]
                for m in range(2):
                    r = 2 * i + m
                    pr = rows(par_a.at[j], 6 * plane + r)
                    pi = rows(par_a.at[j], 8 * plane + r)
                    wr = rows(par_b.at[j], 3 * plane + r)
                    wi = rows(par_b.at[j], 5 * plane + r)
                    sr = excl[j, i, 16 * m : 16 * m + 8, :]
                    si = excl[j, i, 16 * m + 8 : 16 * m + 16, :]
                    for k in range(STEPS):
                        keep = m_keep[k]
                        tr, ti = keep * sr, keep * si
                        sr = pr * tr - pi * ti + v[k]
                        si = pr * ti + pi * tr
                        y[k] = y[k] + (wr * sr - wi * si)
                    for n, bit in enumerate((1, 2, 4)):
                        on = (chunk & bit) > 0
                        br = jnp.where(on, rows(derived.at[j], 2 * n * n_rows + r), one)
                        bi = jnp.where(on, rows(derived.at[j], (2 * n + 1) * n_rows + r), zero)
                        wr, wi = cmul(wr, wi, br, bi)
                    table[j, i, 32 * m : 32 * m + 8, :] = wr
                    table[j, i, 32 * m + 8 : 32 * m + 16, :] = wi
                    wr, wi = cmul(wr, wi, pr, pi)
                    table[j, i, 32 * m + 16 : 32 * m + 24, :] = wr
                    table[j, i, 32 * m + 24 : 32 * m + 32, :] = wi
                for k in range(STEPS):
                    gr[j, i, 8 * k : 8 * k + 8, :] = gate[k] * y[k]
                    gm[j, i, 8 * k : 8 * k + 8, :] = gate[k] * m_first[k]

    def finish(j):
        whole_3(j).wait_recv()

        for i2 in range(width // 256):
            halves = []
            for h in range(2):
                i = 2 * i2 + h
                added = None
                for m in range(2):
                    r = 2 * i + m
                    ir = rows(inflow.at[j, i], m)
                    ii = rows(inflow.at[j, i], 2 + m)
                    a1 = rows(derived.at[j], 10 * n_rows + r)
                    a2 = rows(derived.at[j], 11 * n_rows + r)
                    t = [table[j, i, 32 * m + 8 * n : 32 * m + 8 * n + 8, :] for n in range(4)]
                    older = t[0] * ir - t[1] * ii
                    u = [t[2] * ir - t[3] * ii]
                    for k in range(1, STEPS):
                        u.append(a1 * u[-1] - a2 * older)
                        older = u[-2]
                    added = u if added is None else [a + b for a, b in zip(added, u)]
                halves.append(
                    jnp.concatenate(
                        [
                            gr[j, i, 8 * k : 8 * k + 8, :] + gm[j, i, 8 * k : 8 * k + 8, :] * added[k]
                            for k in range(STEPS)
                        ],
                        axis=0,
                    )
                )
            mixed = jnp.concatenate(halves, axis=1).astype(BF16)
            lane = pl.ds(pl.multiple_of(block[j] * width + i2 * 256, 256), 256)
            obuf[:, lane] = jnp.dot(perm_out[...], mixed, preferred_element_type=F32).astype(BF16)
        columns = pl.ds(pl.multiple_of(block[j] * width, width), width)
        pltpu.make_async_copy(obuf.at[:, columns], out.at[0, :, columns], o_sem).start()

    for j in range(n_dp):
        permute(j)
    products(0)
    for j in range(1, n_dp):
        send_a(j).wait_recv()
        if j == n_dp - 1:
            for n in range(1, n_dp):
                send_b(n).start()
        products(j)
        if j == 1:

            @pl.when(me > 0)
            def _():
                send_h().wait_recv()

            tiles = half // LANES
            for t in range(tiles):
                both = hrecv[:, t * LANES : (t + 1) * LANES].astype(F32)
                hrows[t] = both[:8]
                hrows[tiles + t] = both[8:]
            states(0)
            gather_plane(0)
        states(j)
        gather_plane(j)
    response(0)
    learn_later()
    for j in range(n_dp):
        combine_plane(j)
    for j in range(1, n_dp):
        send_b(j).wait_recv()
        if j < n_dp - 1 or n_dp == 2:
            response(j)
    for j in range(n_dp):
        combine_all(j)
    if n_dp > 2:
        response(n_dp - 1)
    for j in range(n_dp):
        finish(j)

    @pl.when(me + 1 < n_seq)
    def _():
        send_h().wait_send()

    for j in range(1, n_dp):
        send_a(j).wait_send()
    for j in range(1, n_dp):
        send_b(j).wait_send()
    others = pl.ds(0, plane - 1)
    for source, target, sem in ((state, r1, s1_send), (back, inflow, s3_send)):
        remote(source.at[:, others], target.at[:, others], sem, s1_recv.at[0], q_peer[0]).wait_send()
    for count in range(1, n_z):

        @pl.when(n_z - 1 - me_z == count)
        def _():
            those = r2.at[:, pl.ds(0, count)]
            remote(those, those, s2_send, s2_recv.at[0], z_later[0]).wait_send()

    pltpu.make_async_copy(obuf, out.at[0], o_sem).wait()


def local(n_dp, n_seq, streams, short_filter, decay_rate, pole_angle, residue_re, residue_im, skip_gain, doc_starts):
    width = short_filter.shape[2]
    plane = width // LANES
    n_z = n_seq // plane
    n_rows = 2 * plane
    vmem = pltpu.VMEM
    dma = pltpu.SemaphoreType.DMA
    anywhere = pl.BlockSpec(memory_space=pl.ANY)
    return pl.pallas_call(
        functools.partial(kernel, n_dp, n_seq, plane),
        out_shape=jax.ShapeDtypeStruct((1, TOK, streams.shape[3]), BF16),
        in_specs=[anywhere] * 8,
        out_specs=anywhere,
        scratch_shapes=[
            vmem((3, TOK, n_dp * width), BF16),
            vmem((16, n_dp * width // 2), BF16),
            vmem((16, n_dp * width // 2), BF16),
            vmem((16, n_dp * width // 2), F32),
            vmem((n_dp * plane, 8, LANES), F32),
            vmem((n_dp, 3, plane, TOK, LANES), F32),
            vmem((n_dp, plane, 32, LANES), F32),
            vmem((TOK, n_dp * width), BF16),
            vmem((3, 3, width), F32),
            vmem((2, width), F32),
            vmem((2, width), F32),
            vmem((2, width), F32),
            vmem((2, width), F32),
            vmem((1, width), F32),
            vmem((4, n_rows, LANES), F32),
            pltpu.SMEM(doc_starts.shape, jnp.int32),
            vmem((n_dp, 10 * plane, LANES), F32),
            vmem((n_dp, 8 * plane, LANES), F32),
            vmem((n_dp, 16 * n_rows, LANES), F32),
            vmem((TOK, TOK), BF16),
            vmem((TOK, TOK), BF16),
            vmem((STEPS, 8, LANES), F32),
            vmem((STEPS, 8, LANES), F32),
            vmem((2, 8, LANES), F32),
            vmem((STEPS, 8, LANES), F32),
            vmem((3, 8, LANES), F32),
            vmem((2, 8, LANES), F32),
            vmem((n_dp, plane, TOK, LANES), F32),
            vmem((n_dp, plane, TOK, LANES), F32),
            vmem((n_dp, plane, TOK, LANES), F32),
            vmem((n_dp, plane, 32, LANES), F32),
            vmem((n_dp, plane, 64, LANES), F32),
            vmem((n_dp, plane, 4, LANES), F32),
            vmem((n_dp, plane, 4, LANES), F32),
            vmem((n_dp, plane, 4, LANES), F32),
            vmem((n_dp, 4, LANES), F32),
            vmem((n_dp, n_z, 4, LANES), F32),
            vmem((n_dp, plane, 4, LANES), F32),
            vmem((n_dp, plane, 4, LANES), F32),
            dma((7,)),
            dma(()),
            dma((n_dp - 1,)),
            dma((n_dp - 1,)),
            dma((n_dp - 1,)),
            dma((n_dp - 1,)),
            dma(()),
            dma(()),
            dma(()),
            dma((n_dp,)),
            dma(()),
            dma((n_dp,)),
            dma(()),
            dma((n_dp,)),
            dma(()),
            pltpu.SemaphoreType.REGULAR,
        ],
        compiler_params=pltpu.CompilerParams(collective_id=0, has_side_effects=True, vmem_limit_bytes=48 * 2**20),
        name="hyena_modal_scan",
    )(
        *[
            pltpu.with_memory_space_constraint(a, pltpu.HBM)
            for a in (
                streams,
                short_filter,
                decay_rate,
                pole_angle,
                residue_re,
                residue_im,
                skip_gain.reshape(1, width),
                doc_starts,
            )
        ]
    )


def solution(mesh):
    placed = (
        P(None, "dp", "seq", None),
        P(None, None, "dp"),
        P(None, "dp"),
        P(None, "dp"),
        P(None, "dp"),
        P(None, "dp"),
        P("dp"),
        P("dp", None),
    )
    return jax.shard_map(
        functools.partial(local, mesh.shape["dp"], mesh.shape["seq"]),
        mesh=mesh,
        in_specs=placed,
        out_specs=P("dp", "seq", None),
        check_vma=False,
    )
```
